128 devices in a mesh: row: 16 (over y_hi, x, core), col: 8 (over z, y_lo).
Axes of the slice: x: 4, y: 4 (y_hi: 2, y_lo: 2; y = y_hi * 2 + y_lo), z: 4, core: 2. Of those that a mesh axis runs over, the one named last changes fastest.
Arguments:
- orbitals_in: float32 [16384, 256], P(('row', 'col')), may hold values from -6 to 6
- hblocks: bfloat16 [256, 128, 4096], P('row', 'col'), may hold values from -0.046875 to 0.046875
- block_cols: int32 [256, 128], P('row', 'col'), may hold values from 0 to 31, as said below
- live_counts: int32 [256, 8], P('row', 'col'), may hold values from 0 to 16, as said below
- onsite: bfloat16 [256, 4096], P(('row', 'col')), may hold values from -3 to 1, as said below
- cut_low: float32 [1], replicated, may hold values from -1.6 to -1
- top_bound: float32 [1], replicated, may hold values from 2.4 to 3.2
Outputs:
- orbitals: float32 [16384, 256], P(('row', 'col'))
- projected: float32 [256, 256], replicated
The draws below stay inside these ranges and needn't reach their ends.
Inputs may be any that keep to these rules, and one draw needn't show every extreme that they name: `block_cols`: in block row b and column group c the first live_counts[b, c] slots name distinct block columns whose global block index exceeds b (strict upper triangle); the other slots are padding and are ignored. `live_counts`: block row 0 fills all 16 slots of every column group; the last block row has no live slot. `onsite`: every block is symmetric.
All inputs are finite; a program needn't handle non-finite values.
Results may differ from the reference program's by a relative error of at most 0.0008.
The reference program's roundings to bfloat16 on the way count: a program that leaves them out, or rounds other values in their place, can miss the bound.
Values may be sent and summed in bfloat16 or wider, within the bound.
A program may use at most 128 MiB of HBM per device.

```python
import jax
import jax.numpy as jnp
from jax import lax

BS = 64
K = 256
PB = 2
DEG = 3
NBR = 16
NBC = 32
SLOTS = 16
ROW_SLOTS = 128
NB = 256
M = 16384
N_ROW = 16
N_COL = 8


def sparsity_pattern(key):
    folded = jax.random.fold_in(key, 11)
    key_order, key_count = jax.random.split(folded)
    groups = NBR // PB
    block_rows = jnp.arange(NB, dtype=jnp.int32)[:, None, None]
    group_index = jnp.arange(groups, dtype=jnp.int32)[None, :, None]
    local_cols = jnp.arange(NBC, dtype=jnp.int32)[None, None, :]
    global_cols = (local_cols // PB * groups + group_index) * PB + local_cols % PB
    eligible = (global_cols > block_rows).astype(jnp.int32)
    noise = jax.random.randint(key_order, (NB, groups, NBC), 0, 1 << 20)
    scores = (eligible * (1 << 21) + noise) * NBC + local_cols
    ordering = jnp.argsort(-scores, axis=-1).astype(jnp.int32)
    chosen = ordering[:, :, :SLOTS]
    available = jnp.sum(eligible, axis=-1)
    wanted = jax.random.randint(key_count, (NB, groups), 1, SLOTS + 1)
    wanted = wanted.at[0].set(SLOTS)
    counts = jnp.minimum(available, wanted).astype(jnp.int32)
    return (chosen.reshape(NB, groups * SLOTS), counts)


def draw_block_cols(key, part):
    return sparsity_pattern(key)[0]


def draw_live_counts(key, part):
    return sparsity_pattern(key)[1]


def draw_onsite(key, part):
    key_off, key_diag = jax.random.split(jax.random.fold_in(key, 5))
    offdiag = jnp.clip(0.1 * jax.random.normal(key_off, (NB, BS, BS)), -0.45, 0.45)
    energies = jax.random.uniform(key_diag, (NB, BS), minval=-2.5, maxval=0.5)
    offdiag = 0.5 * (offdiag + jnp.swapaxes(offdiag, 1, 2))
    blocks = offdiag + energies[:, :, None] * jnp.eye(BS, dtype=jnp.float32)[None, :, :]
    return blocks.reshape(NB, BS * BS).astype(jnp.bfloat16)


def block_scale(key, extent, cuts, least, top_value):
    def one(dim, blocks):
        steps = jax.random.uniform(jax.random.fold_in(jax.random.fold_in(key, 6), dim), (blocks,), jnp.float32, least / len(cuts), top_value / len(cuts))
        return jnp.repeat(jnp.exp(steps), extent[dim] // blocks).reshape((-1,) + (1,) * (len(extent) - dim - 1))

    level = one(*cuts[0])
    for cut in cuts[1:]:
        level = level * one(*cut)
    return level


def centred(key, extent, width, bound, pieces=(), held_as=jnp.bfloat16):
    factor_of = block_scale(key, extent, pieces, -0.22, 0.18) if pieces else 1.0
    entries = jax.random.normal(key, extent, jnp.float32) * width * factor_of
    return jnp.minimum(jnp.maximum(entries, -bound), bound).astype(held_as)


def setup_inputs(seed: int = 0) -> dict:
    arg_keys = jax.random.split(jax.random.key(seed), 8)
    return {
        "orbitals_in": centred(arg_keys[0], (M, K), 1.0, 6.0, ((0, 128),), jnp.float32),
        "hblocks": centred(arg_keys[1], (NB, ROW_SLOTS, BS * BS), (BS * NB) ** -0.5, 0.046875, ((0, 16), (1, 8))),
        "block_cols": draw_block_cols(jax.random.fold_in(arg_keys[7], 71), 0),
        "live_counts": draw_live_counts(jax.random.fold_in(arg_keys[7], 71), 0),
        "onsite": draw_onsite(jax.random.fold_in(arg_keys[7], 71), 0),
        "cut_low": jnp.clip(jax.random.uniform(arg_keys[5], (1,), jnp.float32, -1.6, -1.0), -1.6, -1.0),
        "top_bound": jnp.clip(jax.random.uniform(arg_keys[6], (1,), jnp.float32, 2.4, 3.2), 2.4, 3.2),
    }


def global_columns(block_cols):
    slot_index = jnp.arange(N_COL * SLOTS, dtype=jnp.int32)
    group_index = slot_index // SLOTS
    return (block_cols // PB * N_COL + group_index[None, :]) * PB + block_cols % PB

def reference(orbitals_in, hblocks, block_cols, live_counts, onsite, cut_low, top_bound):
    gcols = global_columns(block_cols)
    occupied = (jnp.arange(SLOTS, dtype=jnp.int32)[None, None, :] < live_counts[:, :, None]).reshape(NB, N_COL * SLOTS)
    blocks = hblocks.reshape(NB, N_COL * SLOTS, BS, BS) * occupied[:, :, None, None].astype(jnp.bfloat16)
    onsite_blocks = onsite.reshape(NB, BS, BS).astype(jnp.float32)

    def apply(rounded):
        vblocks = rounded.reshape(NB, BS, K)
        onsite_part = jnp.einsum('nab,nbk->nak', onsite_blocks, vblocks.astype(jnp.float32))

        def group(running, group_row):
            offset = group_row * NBR
            hrows = lax.dynamic_slice_in_dim(blocks, offset, NBR, 0).astype(jnp.float32)
            grows = lax.dynamic_slice_in_dim(gcols, offset, NBR, 0)
            gathered = vblocks[grows].astype(jnp.float32)
            own_rows = lax.dynamic_slice_in_dim(vblocks, offset, NBR, 0).astype(jnp.float32)
            direct = jnp.einsum('isab,isbk->iak', hrows, gathered)
            terms = jnp.einsum('isab,iak->isbk', hrows, own_rows)
            column_part = jnp.zeros((NB, BS, K), jnp.float32).at[grows.reshape(-1)].add(terms.reshape(-1, BS, K))
            return (running + column_part, direct)
        column_sum, row_parts = lax.scan(group, jnp.zeros((NB, BS, K), jnp.float32), jnp.arange(N_ROW, dtype=jnp.int32))
        return (onsite_part + row_parts.reshape(NB, BS, K) + column_sum).reshape(M, K)
    centre = 0.5 * (top_bound[0] + cut_low[0])
    halfwidth = 0.5 * (top_bound[0] - cut_low[0])
    previous = orbitals_in
    current = (apply(orbitals_in.astype(jnp.bfloat16)) - centre * orbitals_in) / halfwidth
    for degree in range(DEG - 1):
        following = 2.0 * (apply(current.astype(jnp.bfloat16)) - centre * current) / halfwidth - previous
        previous, current = (current, following)
    rounded = current.astype(jnp.bfloat16)
    image = apply(rounded)
    as_float = rounded.astype(jnp.float32)
    dims = (((0,), (0,)), ((), ()))
    gram_matrix = lax.dot_general(rounded.astype(jnp.float32), rounded.astype(jnp.float32), dims, preferred_element_type=jnp.float32) / M
    cross = lax.dot_general(as_float, image, dims, precision=lax.Precision.HIGHEST)
    ritz_matrix = (cross + cross.T) / (2.0 * M)
    factor = jnp.linalg.cholesky(gram_matrix)
    orbitals = jax.scipy.linalg.solve_triangular(factor, current.T, lower=True).T
    inner = jax.scipy.linalg.solve_triangular(factor, ritz_matrix, lower=True)
    projected = jax.scipy.linalg.solve_triangular(factor, inner.T, lower=True)
    return (orbitals, projected)
```

```python
import jax
import jax.numpy as jnp
from jax import lax
from jax.experimental import pallas as pl
from jax.experimental.pallas import tpu as pltpu
from jax.sharding import PartitionSpec as P

BS = 64
K = 256
PB = 2
DEG = 3
LR = PB * BS
MESH = pl.DeviceIdType.MESH
F32 = jnp.float32
BF16 = jnp.bfloat16

NR = 16
NC = 8
SLAB = K // NR


def build_tile(hblocks, block_cols, live_counts, column_blocks):
    row_blocks, slot_count, _ = hblocks.shape
    occupied = jnp.arange(slot_count, dtype=jnp.int32)[None, :] < live_counts
    selector = (
        block_cols[:, :, None] == jnp.arange(column_blocks, dtype=jnp.int32)[None, None, :]
    ) & occupied[:, :, None]
    blocks = hblocks.reshape(row_blocks, slot_count, BS, BS)
    dense_tile = jnp.einsum(
        "isc,isab->iacb", selector.astype(jnp.bfloat16), blocks, preferred_element_type=jnp.float32
    )
    return dense_tile.astype(jnp.bfloat16).reshape(row_blocks * BS, column_blocks * BS)


def rcopy(src, dst, ssem, rsem, dev):
    return pltpu.make_async_remote_copy(
        src_ref=src, dst_ref=dst, send_sem=ssem, recv_sem=rsem, device_id=dev, device_id_type=MESH
    )


def contract_rows(a, b):
    return lax.dot_general(a, b, (((0,), (0,)), ((), ())), preferred_element_type=F32)


def kernel(
    tile, tile_t, y0, onsite, low, top, y_out, gram_out, ritz_out,
    vc, vr, ms, sr, mx, xr, zs, zr, ys, yr, ls, lr, prev, cur, part, a1, s2, a2,
    ag_s, ag_r, rs_s, rs_r, ar_s, ar_r,
):
    r = lax.axis_index("row")
    c = lax.axis_index("col")
    core = lax.rem(r, 2)
    x = lax.rem(r // 2, 4)
    yh = r // 8
    z = c // 2
    yl = lax.rem(c, 2)
    sib_r = r + 1 - 2 * core
    yhp_r = lax.rem(r + 8, NR)
    ylp_c = c + 1 - 2 * yl
    sib = (sib_r, c)
    yhp = (yhp_r, c)
    ylp = (r, ylp_c)

    def xrow(d, h=None, k=None):
        return (yh if h is None else h) * 8 + lax.rem(x + d + 4, 4) * 2 + (core if k is None else k)

    def zcol(d, l=None):
        return lax.rem(z + d + 4, 4) * 2 + (yl if l is None else l)

    barrier = pltpu.get_barrier_semaphore()

    def greet_row(j, carry):
        pl.semaphore_signal(barrier, inc=1, device_id=(lax.rem(r + j, NR), c), device_id_type=MESH)
        return carry

    def greet_col(j, carry):
        pl.semaphore_signal(barrier, inc=1, device_id=(r, lax.rem(c + j, NC)), device_id_type=MESH)
        return carry

    lax.fori_loop(1, NR, greet_row, 0)
    lax.fori_loop(1, NC, greet_col, 0)
    pl.semaphore_wait(barrier, NR - 1 + NC - 1)

    def gather(t, value):
        vc[t, r] = value
        vr[t, c] = value
        sends = []

        def send(buf, slot, dev, k):
            cp = rcopy(buf.at[t, slot], buf.at[t, slot], ag_s.at[t, k], ag_r.at[t, k], dev)
            cp.start()
            sends.append(cp)

        def arrived(buf, slot, k):
            rcopy(buf.at[t, slot], buf.at[t, slot], ag_s.at[t, k], ag_r.at[t, k], sib).wait_recv()

        send(vr, c, ylp, 5)
        send(vc, r, yhp, 1)
        for d in (2, 1, 3):
            send(vc, r, (xrow(d), c), 1 + d)
            send(vr, c, (r, zcol(d)), 5 + d)
        send(vc, r, sib, 0)
        arrived(vr, ylp_c, 5)
        for d in (2, 1, 3):
            send(vr, ylp_c, (r, zcol(d)), 11 + d)
        arrived(vc, yhp_r, 1)
        for d in (2, 1, 3):
            send(vc, yhp_r, (xrow(d), c), 8 + d)
        send(vc, yhp_r, sib, 15)
        for d in (1, 3, 2):
            arrived(vc, xrow(-d), 1 + d)
            send(vc, xrow(-d), sib, 15 + d)
        for d in (1, 3, 2):
            arrived(vc, xrow(-d, h=1 - yh), 8 + d)
            send(vc, xrow(-d, h=1 - yh), sib, 18 + d)
        for d in (1, 3, 2):
            arrived(vr, zcol(-d), 5 + d)
        for d in (1, 3, 2):
            arrived(vr, zcol(-d, l=1 - yl), 11 + d)

        def finish():
            other = 1 - core
            arrived(vc, sib_r, 0)
            arrived(vc, xrow(0, h=1 - yh, k=other), 15)
            for d in (1, 3, 2):
                arrived(vc, xrow(-d, k=other), 15 + d)
            for d in (1, 3, 2):
                arrived(vc, xrow(-d, h=1 - yh, k=other), 18 + d)

        return sends, finish

    def onsite_part(value):
        return jnp.concatenate(
            [
                jnp.dot(onsite[p], value[p * BS : (p + 1) * BS], preferred_element_type=F32)
                for p in range(PB)
            ],
            axis=0,
        )

    centre = 0.5 * (top[0] + low[0])
    halfwidth = 0.5 * (top[0] - low[0])
    prev[...] = jnp.zeros_like(prev)
    cur[...] = y0[...]

    def degree(t, carry):
        value = cur[...].astype(BF16)
        sends, finish = gather(t, value)

        row_set = vr[t].reshape(NC * LR, K)
        for d in (2, 1, 3, 0):
            for h in range(2):
                at = pl.multiple_of(xrow(d, h=h, k=1 - core) * LR, LR)
                ms[t, d, h] = jnp.dot(tile_t[pl.ds(at, LR), :], row_set, preferred_element_type=F32)
            cp = rcopy(ms.at[t, d], sr.at[t, d], rs_s.at[t, d], rs_r.at[t, d], sib)
            cp.start()
            sends.append(cp)
        for d in (2, 1, 3, 0):
            rcopy(ms.at[t, d], sr.at[t, d], rs_s.at[t, d], rs_r.at[t, d], sib).wait_recv()
            for h in range(2):
                at = pl.multiple_of(xrow(d, h=h) * LR, LR)
                mx[t, d, h] = sr[t, d, h] + jnp.dot(
                    tile_t[pl.ds(at, LR), :], row_set, preferred_element_type=F32
                )
            if d:
                cp = rcopy(
                    mx.at[t, d], xr.at[t, d - 1], rs_s.at[t, 3 + d], rs_r.at[t, 3 + d], (xrow(d), c)
                )
                cp.start()
                sends.append(cp)
        finish()
        portion = vc[t].reshape(NR * LR, K)
        for d in (2, 1, 3, 0):
            at = pl.multiple_of(zcol(d, l=0) * LR, 2 * LR)
            zs[t, d] = jnp.dot(
                tile[pl.ds(at, 2 * LR), :], portion, preferred_element_type=F32
            ).reshape(2, LR, K)
            if d:
                cp = rcopy(
                    zs.at[t, d], zr.at[t, d - 1], rs_s.at[t, 6 + d], rs_r.at[t, 6 + d], (r, zcol(d))
                )
                cp.start()
                sends.append(cp)
        own = onsite_part(value)

        for d in (1, 3, 2):
            rcopy(mx.at[t, d], xr.at[t, d - 1], rs_s.at[t, 3 + d], rs_r.at[t, 3 + d], sib).wait_recv()
        ys[t] = (mx[t, 0, 1 - yh] + xr[t, 0, 1 - yh]) + (xr[t, 1, 1 - yh] + xr[t, 2, 1 - yh])
        cp_y = rcopy(ys.at[t], yr.at[t], rs_s.at[t, 10], rs_r.at[t, 10], yhp)
        cp_y.start()
        for d in (1, 3, 2):
            rcopy(zs.at[t, d], zr.at[t, d - 1], rs_s.at[t, 6 + d], rs_r.at[t, 6 + d], sib).wait_recv()
        ls[t] = (zs[t, 0, 1 - yl] + zr[t, 0, 1 - yl]) + (zr[t, 1, 1 - yl] + zr[t, 2, 1 - yl])
        cp_l = rcopy(ls.at[t], lr.at[t], rs_s.at[t, 11], rs_r.at[t, 11], ylp)
        cp_l.start()
        own += (mx[t, 0, yh] + xr[t, 0, yh]) + (xr[t, 1, yh] + xr[t, 2, yh])
        own += (zs[t, 0, yl] + zr[t, 0, yl]) + (zr[t, 1, yl] + zr[t, 2, yl])
        cp_y.wait_recv()
        own += yr[t]
        cp_l.wait_recv()
        own += lr[t]
        scale = jnp.where(t == 0, 1.0, 2.0).astype(F32)
        now = cur[...]
        following = scale * (own - centre * now) / halfwidth - prev[...]
        prev[...] = now
        cur[...] = following
        for cp in sends:
            cp.wait_send()
        cp_y.wait_send()
        cp_l.wait_send()
        return carry

    lax.fori_loop(0, DEG, degree, 0)
    y_out[...] = cur[...]
    rounded = cur[...].astype(BF16)
    out = (gram_out, ritz_out)

    def to_row(k):
        def step(j, carry):
            slab = pl.multiple_of(lax.rem(r + j, NR) * SLAB, SLAB)
            rcopy(
                part.at[k, pl.ds(slab, SLAB)], a1.at[k, j - 1], ar_s.at[k, 0, j], ar_r.at[k, 0, j],
                (lax.rem(r + j, NR), c),
            ).start()
            return carry

        lax.fori_loop(1, NR, step, 0)

    mine = pl.multiple_of(r * SLAB, SLAB)

    def to_col(k):
        def take(j, total):
            rcopy(
                a1.at[k, j - 1], a1.at[k, j - 1], ar_s.at[k, 0, j], ar_r.at[k, 0, j], sib
            ).wait_recv()
            return total + a1[k, j - 1]

        s2[k] = lax.fori_loop(1, NR, take, part[k, pl.ds(mine, SLAB), :])

        def step(j, carry):
            rcopy(
                s2.at[k], a2.at[k, j - 1], ar_s.at[k, 1, j], ar_r.at[k, 1, j],
                (r, lax.rem(c + j, NC)),
            ).start()
            return carry

        lax.fori_loop(1, NC, step, 0)

    def spread(k):
        def place(j, carry):
            rcopy(
                a2.at[k, j - 1], a2.at[k, j - 1], ar_s.at[k, 1, j], ar_r.at[k, 1, j], sib
            ).wait_recv()
            return carry

        lax.fori_loop(1, NC, place, 0)
        total = jnp.zeros((SLAB, K), F32)
        for i in range(NC):
            j = lax.rem(c - i + NC, NC)
            other = a2[k, jnp.maximum(j - 1, 0)]
            total = total + jnp.where(j == 0, s2[k], other)
        out[k][pl.ds(mine, SLAB), :] = total

        def step(j, carry):
            rcopy(
                out[k].at[pl.ds(mine, SLAB)], out[k].at[pl.ds(mine, SLAB)],
                ar_s.at[k, 2, j], ar_r.at[k, 2, j], (lax.rem(r + j, NR), c),
            ).start()
            return carry

        lax.fori_loop(1, NR, step, 0)

    def collect(k):
        def step(j, carry):
            there = pl.multiple_of(lax.rem(r - j + NR, NR) * SLAB, SLAB)
            rcopy(
                out[k].at[pl.ds(there, SLAB)], out[k].at[pl.ds(there, SLAB)],
                ar_s.at[k, 2, j], ar_r.at[k, 2, j], sib,
            ).wait_recv()
            return carry

        lax.fori_loop(1, NR, step, 0)

    def settle(k):
        def step(phase):
            def inner(j, carry):
                rcopy(
                    s2.at[k], s2.at[k], ar_s.at[k, phase, j], ar_r.at[k, phase, j], sib
                ).wait_send()
                return carry

            return inner

        lax.fori_loop(1, NR, step(0), 0)
        lax.fori_loop(1, NC, step(1), 0)
        lax.fori_loop(1, NR, step(2), 0)

    part[0] = contract_rows(rounded, rounded)
    to_row(0)
    sends, finish = gather(DEG, rounded)
    to_col(0)
    own = 0.5 * onsite_part(rounded)
    total = jnp.zeros((K, K), F32)

    def three(rows, image):
        high = image.astype(BF16)
        rest = image - high.astype(F32)
        mid = rest.astype(BF16)
        tail = (rest - mid.astype(F32)).astype(BF16)
        return contract_rows(rows, high) + (contract_rows(rows, mid) + contract_rows(rows, tail))

    finish()
    portion = vc[DEG].reshape(NR * LR, K)
    part[1] = three(rounded, own)
    for i in range(NC // 2):
        image = jnp.dot(tile[i * 2 * LR : (i + 1) * 2 * LR, :], portion, preferred_element_type=F32)
        part[1] += three(vr[DEG, 2 * i : 2 * i + 2].reshape(2 * LR, K), image)
    to_row(1)
    spread(0)
    to_col(1)
    collect(0)
    spread(1)
    collect(1)
    for cp in sends:
        cp.wait_send()
    settle(0)
    settle(1)


def local(orbitals_in, hblocks, block_cols, live_counts, onsite, cut_low, top_bound):
    dense_tile = build_tile(hblocks, block_cols, live_counts, NR * PB)
    vmem = pl.BlockSpec(memory_space=pltpu.VMEM)
    smem = pl.BlockSpec(memory_space=pltpu.SMEM)
    block = (LR, K)
    dma = pltpu.SemaphoreType.DMA
    current, gram_total, half_total = pl.pallas_call(
        kernel,
        out_shape=(
            jax.ShapeDtypeStruct(block, F32),
            jax.ShapeDtypeStruct((K, K), F32),
            jax.ShapeDtypeStruct((K, K), F32),
        ),
        in_specs=[vmem, vmem, vmem, vmem, smem, smem],
        out_specs=(vmem, vmem, vmem),
        scratch_shapes=[
            pltpu.VMEM((DEG + 1, NR) + block, BF16),
            pltpu.VMEM((DEG + 1, NC) + block, BF16),
            pltpu.VMEM((DEG, 4, 2) + block, F32),
            pltpu.VMEM((DEG, 4, 2) + block, F32),
            pltpu.VMEM((DEG, 4, 2) + block, F32),
            pltpu.VMEM((DEG, 3, 2) + block, F32),
            pltpu.VMEM((DEG, 4, 2) + block, F32),
            pltpu.VMEM((DEG, 3, 2) + block, F32),
            pltpu.VMEM((DEG,) + block, F32),
            pltpu.VMEM((DEG,) + block, F32),
            pltpu.VMEM((DEG,) + block, F32),
            pltpu.VMEM((DEG,) + block, F32),
            pltpu.VMEM(block, F32),
            pltpu.VMEM(block, F32),
            pltpu.VMEM((2, K, K), F32),
            pltpu.VMEM((2, NR - 1, SLAB, K), F32),
            pltpu.VMEM((2, SLAB, K), F32),
            pltpu.VMEM((2, NC - 1, SLAB, K), F32),
            dma((DEG + 1, 22)),
            dma((DEG + 1, 22)),
            dma((DEG, 12)),
            dma((DEG, 12)),
            dma((2, 3, NR)),
            dma((2, 3, NR)),
        ],
        compiler_params=pltpu.CompilerParams(
            collective_id=0, has_side_effects=True, vmem_limit_bytes=60 * 1024 * 1024
        ),
        name="filter_and_project",
    )(dense_tile, dense_tile.T, orbitals_in, onsite.reshape(PB, BS, BS), cut_low, top_bound)
    total_rows = NR * NC * LR
    gram_matrix = gram_total / total_rows
    ritz_matrix = (half_total + half_total.T) / total_rows
    factor = jnp.linalg.cholesky(gram_matrix)
    orbitals = jax.scipy.linalg.solve_triangular(factor, current.T, lower=True).T
    inner = jax.scipy.linalg.solve_triangular(factor, ritz_matrix, lower=True)
    projected = jax.scipy.linalg.solve_triangular(factor, inner.T, lower=True)
    return (orbitals, projected)


def solution(mesh):
    placed = (
        P(("row", "col"), None),
        P("row", "col", None),
        P("row", "col"),
        P("row", "col"),
        P(("row", "col"), None),
        P(),
        P(),
    )
    return jax.shard_map(
        local, mesh=mesh, in_specs=placed, out_specs=(P(("row", "col"), None), P()), check_vma=False
    )
```

```python
import jax
import jax.numpy as jnp
from jax import lax
from jax.experimental import pallas as pl
from jax.experimental.pallas import tpu as pltpu
from jax.sharding import PartitionSpec as P

BS = 64
K = 256
PB = 2
DEG = 3
LR = PB * BS
MESH = pl.DeviceIdType.MESH
F32 = jnp.float32
BF16 = jnp.bfloat16

NR = 16
NC = 8
SLAB = K // NR
CB = 64
STEP = 8
HIGH = lax.Precision.HIGHEST


def build_tile(hblocks, block_cols, live_counts, column_blocks):
    row_blocks, slot_count, _ = hblocks.shape
    occupied = jnp.arange(slot_count, dtype=jnp.int32)[None, :] < live_counts
    selector = (
        block_cols[:, :, None] == jnp.arange(column_blocks, dtype=jnp.int32)[None, None, :]
    ) & occupied[:, :, None]
    blocks = hblocks.reshape(row_blocks, slot_count, BS, BS)
    dense_tile = jnp.einsum(
        "isc,isab->iacb", selector.astype(jnp.bfloat16), blocks, preferred_element_type=jnp.float32
    )
    return dense_tile.astype(jnp.bfloat16).reshape(row_blocks * BS, column_blocks * BS)


def rcopy(src, dst, ssem, rsem, dev):
    return pltpu.make_async_remote_copy(
        src_ref=src, dst_ref=dst, send_sem=ssem, recv_sem=rsem, device_id=dev, device_id_type=MESH
    )


def contract_rows(a, b):
    return lax.dot_general(a, b, (((0,), (0,)), ((), ())), preferred_element_type=F32)


def kernel(
    tile, tile_t, y0, onsite, low, top, y_out, gram_out, ritz_out,
    vc, vr, ms, sr, mx, xr, zs, zr, ys, yr, ls, lr, prev, cur, part, a1, s2, a2,
    ag_s, ag_r, rs_s, rs_r, ar_s, ar_r,
):
    r = lax.axis_index("row")
    c = lax.axis_index("col")
    core = lax.rem(r, 2)
    x = lax.rem(r // 2, 4)
    yh = r // 8
    z = c // 2
    yl = lax.rem(c, 2)
    sib_r = r + 1 - 2 * core
    yhp_r = lax.rem(r + 8, NR)
    ylp_c = c + 1 - 2 * yl
    sib = (sib_r, c)
    yhp = (yhp_r, c)
    ylp = (r, ylp_c)

    def xrow(d, h=None, k=None):
        return (yh if h is None else h) * 8 + lax.rem(x + d + 4, 4) * 2 + (core if k is None else k)

    def zcol(d, l=None):
        return lax.rem(z + d + 4, 4) * 2 + (yl if l is None else l)

    barrier = pltpu.get_barrier_semaphore()

    def greet_row(j, carry):
        pl.semaphore_signal(barrier, inc=1, device_id=(lax.rem(r + j, NR), c), device_id_type=MESH)
        return carry

    def greet_col(j, carry):
        pl.semaphore_signal(barrier, inc=1, device_id=(r, lax.rem(c + j, NC)), device_id_type=MESH)
        return carry

    lax.fori_loop(1, NR, greet_row, 0)
    lax.fori_loop(1, NC, greet_col, 0)
    pl.semaphore_wait(barrier, NR - 1 + NC - 1)

    def gather(t, value):
        vc[t, r] = value
        vr[t, c] = value
        sends = []

        def send(buf, slot, dev, k):
            cp = rcopy(buf.at[t, slot], buf.at[t, slot], ag_s.at[t, k], ag_r.at[t, k], dev)
            cp.start()
            sends.append(cp)

        def arrived(buf, slot, k):
            rcopy(buf.at[t, slot], buf.at[t, slot], ag_s.at[t, k], ag_r.at[t, k], sib).wait_recv()

        send(vr, c, ylp, 5)
        send(vc, r, yhp, 1)
        for d in (2, 1, 3):
            send(vc, r, (xrow(d), c), 1 + d)
            send(vr, c, (r, zcol(d)), 5 + d)
        send(vc, r, sib, 0)
        arrived(vr, ylp_c, 5)
        for d in (2, 1, 3):
            send(vr, ylp_c, (r, zcol(d)), 11 + d)
        arrived(vc, yhp_r, 1)
        for d in (2, 1, 3):
            send(vc, yhp_r, (xrow(d), c), 8 + d)
        send(vc, yhp_r, sib, 15)
        for d in (1, 3, 2):
            arrived(vc, xrow(-d), 1 + d)
            send(vc, xrow(-d), sib, 15 + d)
        for d in (1, 3, 2):
            arrived(vc, xrow(-d, h=1 - yh), 8 + d)
            send(vc, xrow(-d, h=1 - yh), sib, 18 + d)
        for d in (1, 3, 2):
            arrived(vr, zcol(-d), 5 + d)
        for d in (1, 3, 2):
            arrived(vr, zcol(-d, l=1 - yl), 11 + d)

        def finish():
            other = 1 - core
            arrived(vc, sib_r, 0)
            arrived(vc, xrow(0, h=1 - yh, k=other), 15)
            for d in (1, 3, 2):
                arrived(vc, xrow(-d, k=other), 15 + d)
            for d in (1, 3, 2):
                arrived(vc, xrow(-d, h=1 - yh, k=other), 18 + d)

        return sends, finish

    def onsite_part(value):
        return jnp.concatenate(
            [
                jnp.dot(onsite[p], value[p * BS : (p + 1) * BS], preferred_element_type=F32)
                for p in range(PB)
            ],
            axis=0,
        )

    centre = 0.5 * (top[0] + low[0])
    halfwidth = 0.5 * (top[0] - low[0])
    prev[...] = jnp.zeros_like(prev)
    cur[...] = y0[...]

    def degree(t, carry):
        value = cur[...].astype(BF16)
        sends, finish = gather(t, value)

        row_set = vr[t].reshape(NC * LR, K)
        for d in (2, 1, 3, 0):
            for h in range(2):
                at = pl.multiple_of(xrow(d, h=h, k=1 - core) * LR, LR)
                ms[t, d, h] = jnp.dot(tile_t[pl.ds(at, LR), :], row_set, preferred_element_type=F32)
            cp = rcopy(ms.at[t, d], sr.at[t, d], rs_s.at[t, d], rs_r.at[t, d], sib)
            cp.start()
            sends.append(cp)
        for d in (2, 1, 3, 0):
            rcopy(ms.at[t, d], sr.at[t, d], rs_s.at[t, d], rs_r.at[t, d], sib).wait_recv()
            for h in range(2):
                at = pl.multiple_of(xrow(d, h=h) * LR, LR)
                mx[t, d, h] = sr[t, d, h] + jnp.dot(
                    tile_t[pl.ds(at, LR), :], row_set, preferred_element_type=F32
                )
            if d:
                cp = rcopy(
                    mx.at[t, d], xr.at[t, d - 1], rs_s.at[t, 3 + d], rs_r.at[t, 3 + d], (xrow(d), c)
                )
                cp.start()
                sends.append(cp)
        finish()
        portion = vc[t].reshape(NR * LR, K)
        for d in (2, 1, 3, 0):
            at = pl.multiple_of(zcol(d, l=0) * LR, 2 * LR)
            zs[t, d] = jnp.dot(
                tile[pl.ds(at, 2 * LR), :], portion, preferred_element_type=F32
            ).reshape(2, LR, K)
            if d:
                cp = rcopy(
                    zs.at[t, d], zr.at[t, d - 1], rs_s.at[t, 6 + d], rs_r.at[t, 6 + d], (r, zcol(d))
                )
                cp.start()
                sends.append(cp)
        own = onsite_part(value)

        for d in (1, 3, 2):
            rcopy(mx.at[t, d], xr.at[t, d - 1], rs_s.at[t, 3 + d], rs_r.at[t, 3 + d], sib).wait_recv()
        ys[t] = (mx[t, 0, 1 - yh] + xr[t, 0, 1 - yh]) + (xr[t, 1, 1 - yh] + xr[t, 2, 1 - yh])
        cp_y = rcopy(ys.at[t], yr.at[t], rs_s.at[t, 10], rs_r.at[t, 10], yhp)
        cp_y.start()
        for d in (1, 3, 2):
            rcopy(zs.at[t, d], zr.at[t, d - 1], rs_s.at[t, 6 + d], rs_r.at[t, 6 + d], sib).wait_recv()
        ls[t] = (zs[t, 0, 1 - yl] + zr[t, 0, 1 - yl]) + (zr[t, 1, 1 - yl] + zr[t, 2, 1 - yl])
        cp_l = rcopy(ls.at[t], lr.at[t], rs_s.at[t, 11], rs_r.at[t, 11], ylp)
        cp_l.start()
        own += (mx[t, 0, yh] + xr[t, 0, yh]) + (xr[t, 1, yh] + xr[t, 2, yh])
        own += (zs[t, 0, yl] + zr[t, 0, yl]) + (zr[t, 1, yl] + zr[t, 2, yl])
        cp_y.wait_recv()
        own += yr[t]
        cp_l.wait_recv()
        own += lr[t]
        scale = jnp.where(t == 0, 1.0, 2.0).astype(F32)
        now = cur[...]
        following = scale * (own - centre * now) / halfwidth - prev[...]
        prev[...] = now
        cur[...] = following
        for cp in sends:
            cp.wait_send()
        cp_y.wait_send()
        cp_l.wait_send()
        return carry

    lax.fori_loop(0, DEG, degree, 0)
    y_out[...] = cur[...]
    rounded = cur[...].astype(BF16)
    out = (gram_out, ritz_out)

    def to_row(k):
        def step(j, carry):
            slab = pl.multiple_of(lax.rem(r + j, NR) * SLAB, SLAB)
            rcopy(
                part.at[k, pl.ds(slab, SLAB)], a1.at[k, j - 1], ar_s.at[k, 0, j], ar_r.at[k, 0, j],
                (lax.rem(r + j, NR), c),
            ).start()
            return carry

        lax.fori_loop(1, NR, step, 0)

    mine = pl.multiple_of(r * SLAB, SLAB)

    def to_col(k):
        def take(j, total):
            rcopy(
                a1.at[k, j - 1], a1.at[k, j - 1], ar_s.at[k, 0, j], ar_r.at[k, 0, j], sib
            ).wait_recv()
            return total + a1[k, j - 1]

        s2[k] = lax.fori_loop(1, NR, take, part[k, pl.ds(mine, SLAB), :])

        def step(j, carry):
            rcopy(
                s2.at[k], a2.at[k, j - 1], ar_s.at[k, 1, j], ar_r.at[k, 1, j],
                (r, lax.rem(c + j, NC)),
            ).start()
            return carry

        lax.fori_loop(1, NC, step, 0)

    def spread(k):
        def place(j, carry):
            rcopy(
                a2.at[k, j - 1], a2.at[k, j - 1], ar_s.at[k, 1, j], ar_r.at[k, 1, j], sib
            ).wait_recv()
            return carry

        lax.fori_loop(1, NC, place, 0)
        total = jnp.zeros((SLAB, K), F32)
        for i in range(NC):
            j = lax.rem(c - i + NC, NC)
            other = a2[k, jnp.maximum(j - 1, 0)]
            total = total + jnp.where(j == 0, s2[k], other)
        out[k][pl.ds(mine, SLAB), :] = total

        def step(j, carry):
            rcopy(
                out[k].at[pl.ds(mine, SLAB)], out[k].at[pl.ds(mine, SLAB)],
                ar_s.at[k, 2, j], ar_r.at[k, 2, j], (lax.rem(r + j, NR), c),
            ).start()
            return carry

        lax.fori_loop(1, NR, step, 0)

    def collect(k):
        def step(j, carry):
            there = pl.multiple_of(lax.rem(r - j + NR, NR) * SLAB, SLAB)
            rcopy(
                out[k].at[pl.ds(there, SLAB)], out[k].at[pl.ds(there, SLAB)],
                ar_s.at[k, 2, j], ar_r.at[k, 2, j], sib,
            ).wait_recv()
            return carry

        lax.fori_loop(1, NR, step, 0)

    def settle(k):
        def step(phase):
            def inner(j, carry):
                rcopy(
                    s2.at[k], s2.at[k], ar_s.at[k, phase, j], ar_r.at[k, phase, j], sib
                ).wait_send()
                return carry

            return inner

        lax.fori_loop(1, NR, step(0), 0)
        lax.fori_loop(1, NC, step(1), 0)
        lax.fori_loop(1, NR, step(2), 0)

    part[0] = contract_rows(rounded, rounded)
    to_row(0)
    sends, finish = gather(DEG, rounded)
    to_col(0)
    own = 0.5 * onsite_part(rounded)
    total = jnp.zeros((K, K), F32)

    def three(rows, image):
        high = image.astype(BF16)
        rest = image - high.astype(F32)
        mid = rest.astype(BF16)
        tail = (rest - mid.astype(F32)).astype(BF16)
        return contract_rows(rows, high) + (contract_rows(rows, mid) + contract_rows(rows, tail))

    finish()
    portion = vc[DEG].reshape(NR * LR, K)
    part[1] = three(rounded, own)
    for i in range(NC // 2):
        image = jnp.dot(tile[i * 2 * LR : (i + 1) * 2 * LR, :], portion, preferred_element_type=F32)
        part[1] += three(vr[DEG, 2 * i : 2 * i + 2].reshape(2 * LR, K), image)
    to_row(1)
    spread(0)
    to_col(1)
    collect(0)
    spread(1)
    collect(1)
    for cp in sends:
        cp.wait_send()
    settle(0)
    settle(1)


def dot_f32(a, b, left, right):
    return lax.dot_general(a, b, (((left,), (right,)), ((), ())), precision=HIGH, preferred_element_type=F32)


def dot_nn(a, b):
    return dot_f32(a, b, 1, 0)


def dot_nt(a, b):
    return dot_f32(a, b, 1, 1)


def dot_tn(a, b):
    return dot_f32(a, b, 0, 0)


def inverse_factor(block):
    rows = lax.broadcasted_iota(jnp.int32, (CB, 2 * CB), 0)
    lanes = lax.broadcasted_iota(jnp.int32, (CB, 2 * CB), 1)
    unit = jnp.where(lanes == rows + CB, 1.0, 0.0).astype(F32)
    x = jnp.where(lanes < CB, jnp.concatenate([block, block], axis=1), unit)
    for s in range(0, CB, STEP):
        col = [jnp.broadcast_to(x[:, s + j : s + j + 1], (CB, 2 * CB)) for j in range(STEP)]
        row = [x[s + j : s + j + 1, :] for j in range(STEP)]
        for j in range(STEP):
            d = col[j][s + j : s + j + 1, :]
            q = lax.rsqrt(d)
            col[j] = col[j] * q
            row[j] = row[j] * q
            for m in range(j + 1, STEP):
                f = col[j][s + m : s + m + 1, :]
                col[m] = col[m] - col[j] * f
                row[m] = row[m] - row[j] * f
        change = col[0] * row[0]
        for j in range(1, STEP):
            change = change + col[j] * row[j]
        x = jnp.where(rows >= s + STEP, x - change, x)
        for j in range(STEP):
            x = jnp.where(rows == s + j, row[j], x)
    return x[:, CB:]


def invert(a, b):
    b[...] = jnp.zeros_like(b)
    for k in range(0, K, CB):
        e = k + CB
        inv = inverse_factor(a[k:e, k:e])
        if k:
            b[k:e, :k] = dot_nn(inv, b[k:e, :k])
        b[k:e, k:e] = inv
        if e < K:
            u = dot_nn(inv, a[k:e, e:])
            a[e:, e:] = a[e:, e:] - dot_tn(u, u)
            b[e:, :e] = b[e:, :e] - dot_tn(u, b[k:e, :e])


def finish_kernel(cur, gram, half, orb, proj, a, b):
    scale = 1.0 / (NR * NC * LR)
    a[...] = gram[...] * scale
    invert(a, b)
    w = b[...]
    orb[...] = dot_nt(cur[...], w)
    s = half[...] * scale
    proj[...] = dot_nt(dot_nn(w, s) + dot_nt(w, s), w)


def local(orbitals_in, hblocks, block_cols, live_counts, onsite, cut_low, top_bound):
    dense_tile = build_tile(hblocks, block_cols, live_counts, NR * PB)
    vmem = pl.BlockSpec(memory_space=pltpu.VMEM)
    smem = pl.BlockSpec(memory_space=pltpu.SMEM)
    block = (LR, K)
    dma = pltpu.SemaphoreType.DMA
    current, gram_total, half_total = pl.pallas_call(
        kernel,
        out_shape=(
            jax.ShapeDtypeStruct(block, F32),
            jax.ShapeDtypeStruct((K, K), F32),
            jax.ShapeDtypeStruct((K, K), F32),
        ),
        in_specs=[vmem, vmem, vmem, vmem, smem, smem],
        out_specs=(vmem, vmem, vmem),
        scratch_shapes=[
            pltpu.VMEM((DEG + 1, NR) + block, BF16),
            pltpu.VMEM((DEG + 1, NC) + block, BF16),
            pltpu.VMEM((DEG, 4, 2) + block, F32),
            pltpu.VMEM((DEG, 4, 2) + block, F32),
            pltpu.VMEM((DEG, 4, 2) + block, F32),
            pltpu.VMEM((DEG, 3, 2) + block, F32),
            pltpu.VMEM((DEG, 4, 2) + block, F32),
            pltpu.VMEM((DEG, 3, 2) + block, F32),
            pltpu.VMEM((DEG,) + block, F32),
            pltpu.VMEM((DEG,) + block, F32),
            pltpu.VMEM((DEG,) + block, F32),
            pltpu.VMEM((DEG,) + block, F32),
            pltpu.VMEM(block, F32),
            pltpu.VMEM(block, F32),
            pltpu.VMEM((2, K, K), F32),
            pltpu.VMEM((2, NR - 1, SLAB, K), F32),
            pltpu.VMEM((2, SLAB, K), F32),
            pltpu.VMEM((2, NC - 1, SLAB, K), F32),
            dma((DEG + 1, 22)),
            dma((DEG + 1, 22)),
            dma((DEG, 12)),
            dma((DEG, 12)),
            dma((2, 3, NR)),
            dma((2, 3, NR)),
        ],
        compiler_params=pltpu.CompilerParams(
            collective_id=0, has_side_effects=True, vmem_limit_bytes=60 * 1024 * 1024
        ),
        name="filter_and_project",
    )(dense_tile, dense_tile.T, orbitals_in, onsite.reshape(PB, BS, BS), cut_low, top_bound)
    return pl.pallas_call(
        finish_kernel,
        out_shape=(jax.ShapeDtypeStruct(block, F32), jax.ShapeDtypeStruct((K, K), F32)),
        scratch_shapes=[pltpu.VMEM((K, K), F32)] * 2,
        name="orthonormalize",
    )(current, gram_total, half_total)


def solution(mesh):
    placed = (
        P(("row", "col"), None),
        P("row", "col", None),
        P("row", "col"),
        P("row", "col"),
        P(("row", "col"), None),
        P(),
        P(),
    )
    return jax.shard_map(
        local, mesh=mesh, in_specs=placed, out_specs=(P(("row", "col"), None), P()), check_vma=False
    )
```

```python
import jax
import jax.numpy as jnp
from jax import lax
from jax.experimental import pallas as pl
from jax.experimental.pallas import tpu as pltpu
from jax.sharding import PartitionSpec as P

BS = 64
K = 256
PB = 2
DEG = 3
LR = PB * BS
MESH = pl.DeviceIdType.MESH
F32 = jnp.float32
BF16 = jnp.bfloat16

NR = 16
NC = 8
SLAB = K // NR
CB = 64
STEP = 8
HIGH = lax.Precision.HIGHEST


def rcopy(src, dst, ssem, rsem, dev):
    return pltpu.make_async_remote_copy(
        src_ref=src, dst_ref=dst, send_sem=ssem, recv_sem=rsem, device_id=dev, device_id_type=MESH
    )


def product(a, b, left, right):
    return lax.dot_general(a, b, (((left,), (right,)), ((), ())), preferred_element_type=F32)


def build(blocks, cols, live, pick, tile):
    slots = lax.broadcasted_iota(jnp.int32, cols.shape, 1)
    wanted = jnp.where(slots < live[...], cols[...], -9).astype(F32).astype(BF16)
    count = cols.shape[1]
    depth = 4 * 8 * count
    lane = lax.broadcasted_iota(jnp.int32, (count, depth), 1)
    row = lax.broadcasted_iota(jnp.int32, (count, depth), 0)
    spread = jnp.where(lax.rem(lane, count) == row, 1.0, 0.0).astype(BF16)
    column = product(wanted, spread, 1, 0)
    column = column - lax.rem(lane // (8 * count), 2).astype(F32)

    high = lax.broadcasted_iota(jnp.int32, pick.shape, 0)
    deep = lax.broadcasted_iota(jnp.int32, pick.shape, 1)
    match = lax.rem(high, 16) == 2 * lax.rem(deep // count, 8) + deep // (16 * count)
    pick[...] = jnp.where(match, 2 * (high // 16), -99).astype(F32)
    first = lax.broadcasted_iota(jnp.int32, (8 * count, 2 * BS), 1) < BS
    none = jnp.zeros((8 * count, 2 * BS), BF16)
    return column, first, none


def build_row(i, blocks, column_ref, pick, first, none, tile):
    place = jnp.where(pick[...] == column_ref[pl.ds(i, 1), :], 1.0, 0.0).astype(BF16)
    for half in range(2):
        sides = []
        for p in (2 * half, 2 * half + 1):
            at = [(p * 8 + m) * 2 * BS for m in range(8)]
            plain = jnp.concatenate([blocks[i, :, a : a + 2 * BS] for a in at], axis=0)
            swapped = jnp.concatenate([plain[:, BS:], plain[:, :BS]], axis=1)
            sides.append(
                jnp.concatenate(
                    [
                        jnp.where(first, plain, none),
                        jnp.where(first, none, swapped),
                        jnp.where(first, swapped, none),
                        jnp.where(first, none, plain),
                    ],
                    axis=0,
                )
            )
        rows = product(place, jnp.concatenate(sides, axis=1), 1, 0).astype(BF16)
        for p in range(2):
            at = pl.multiple_of(i * BS + (2 * half + p) * 16, 16)
            for g in range(NR):
                tile[pl.ds(at, 16), g * LR : (g + 1) * LR] = rows[
                    g * 16 : (g + 1) * 16, p * LR : (p + 1) * LR
                ]


def kernel(
    hblocks, cols, live, y0, onsite, low, top, y_out, gram_out, ritz_out,
    tile, blocks, pick, column, diag,
    vc, vr, ms, sr, mx, xr, zs, zr, ys, yr, ls, lr, prev, cur, part, a1, s2, a2,
    ag_s, ag_r, rs_s, rs_r, ar_s, ar_r, load,
):
    fetch = pltpu.make_async_copy(hblocks, blocks, load)
    fetch.start()
    r = lax.axis_index("row")
    c = lax.axis_index("col")
    core = lax.rem(r, 2)
    x = lax.rem(r // 2, 4)
    yh = r // 8
    z = c // 2
    yl = lax.rem(c, 2)
    sib_r = r + 1 - 2 * core
    yhp_r = lax.rem(r + 8, NR)
    ylp_c = c + 1 - 2 * yl
    sib = (sib_r, c)
    yhp = (yhp_r, c)
    ylp = (r, ylp_c)

    def xrow(d, h=None, k=None):
        return (yh if h is None else h) * 8 + lax.rem(x + d + 4, 4) * 2 + (core if k is None else k)

    def zcol(d, l=None):
        return lax.rem(z + d + 4, 4) * 2 + (yl if l is None else l)

    def part_of(buf, t, slot):
        return buf.at[t, :, pl.ds(pl.multiple_of(slot * LR, LR), LR)]

    barrier = pltpu.get_barrier_semaphore()

    def greet_row(j, carry):
        pl.semaphore_signal(barrier, inc=1, device_id=(lax.rem(r + j, NR), c), device_id_type=MESH)
        return carry

    def greet_col(j, carry):
        pl.semaphore_signal(barrier, inc=1, device_id=(r, lax.rem(c + j, NC)), device_id_type=MESH)
        return carry

    lax.fori_loop(1, NR, greet_row, 0)
    lax.fori_loop(1, NC, greet_col, 0)

    cur[...] = y0[...].T
    prev[...] = jnp.zeros_like(prev)
    diag[...] = jnp.zeros_like(diag)
    for p in range(PB):
        diag[p * BS : (p + 1) * BS, p * BS : (p + 1) * BS] = onsite[p]
    pl.semaphore_wait(barrier, NR - 1 + NC - 1)

    def gather(t, value, between=None):
        vc[t, :, pl.ds(pl.multiple_of(r * LR, LR), LR)] = value
        vr[t, :, pl.ds(pl.multiple_of(c * LR, LR), LR)] = value
        sends = []

        def send(buf, slot, dev, k):
            cp = rcopy(
                part_of(buf, t, slot), part_of(buf, t, slot), ag_s.at[t, k], ag_r.at[t, k], dev
            )
            cp.start()
            sends.append(cp)

        def arrived(buf, slot, k):
            rcopy(
                part_of(buf, t, slot), part_of(buf, t, slot), ag_s.at[t, k], ag_r.at[t, k], sib
            ).wait_recv()

        send(vr, c, ylp, 5)
        send(vc, r, yhp, 1)
        for d in (2, 1, 3):
            send(vc, r, (xrow(d), c), 1 + d)
            send(vr, c, (r, zcol(d)), 5 + d)
        send(vc, r, sib, 0)
        arrived(vr, ylp_c, 5)
        for d in (2, 1, 3):
            send(vr, ylp_c, (r, zcol(d)), 11 + d)
        arrived(vc, yhp_r, 1)
        for d in (2, 1, 3):
            send(vc, yhp_r, (xrow(d), c), 8 + d)
        send(vc, yhp_r, sib, 15)
        for d in (1, 3, 2):
            arrived(vc, xrow(-d), 1 + d)
            send(vc, xrow(-d), sib, 15 + d)
        for d in (1, 3, 2):
            arrived(vc, xrow(-d, h=1 - yh), 8 + d)
            send(vc, xrow(-d, h=1 - yh), sib, 18 + d)
        for d in (1, 3, 2):
            arrived(vr, zcol(-d), 5 + d)
        for d in (1, 3, 2):
            arrived(vr, zcol(-d, l=1 - yl), 11 + d)

        def finish():
            other = 1 - core
            arrived(vc, sib_r, 0)
            arrived(vc, xrow(0, h=1 - yh, k=other), 15)
            for d in (1, 3, 2):
                arrived(vc, xrow(-d, k=other), 15 + d)
            for d in (1, 3, 2):
                arrived(vc, xrow(-d, h=1 - yh, k=other), 18 + d)

        return sends, finish

    centre = 0.5 * (top[0] + low[0])
    halfwidth = 0.5 * (top[0] - low[0])

    def settle_sends(sends):
        for cp in sends:
            cp.wait_send()

    def degree(t, carry):
        value = cur[...].astype(BF16)
        sends, finish = gather(t, value)

        @pl.when(t == 0)
        def _():
            fetch.wait()
            spread, first, none = build(blocks, cols, live, pick, tile)
            column[...] = spread

            def one(i, inner):
                build_row(i, blocks, column, pick, first, none, tile)
                return inner

            lax.fori_loop(0, hblocks.shape[0], one, 0)

        def mirror(d):
            for h in range(2):
                at = pl.multiple_of(xrow(d, h=h, k=0) * LR, 2 * LR)
                both = product(vr[t], tile[:, pl.ds(at, 2 * LR)], 1, 0)
                ms[t, d, 0, h] = both[:, :LR]
                ms[t, d, 1, h] = both[:, LR:]
            cp = rcopy(ms.at[t, d, 1 - core], sr.at[t, d], rs_s.at[t, d], rs_r.at[t, d], sib)
            cp.start()
            sends.append(cp)

        def mirror_on(d):
            rcopy(ms.at[t, d, core], sr.at[t, d], rs_s.at[t, d], rs_r.at[t, d], sib).wait_recv()
            mx[t, d] = sr[t, d] + ms[t, d, core]
            if d:
                cp = rcopy(
                    mx.at[t, d], xr.at[t, d - 1], rs_s.at[t, 3 + d], rs_r.at[t, 3 + d], (xrow(d), c)
                )
                cp.start()
                sends.append(cp)

        def direct(d):
            at = pl.multiple_of(zcol(d, l=0) * LR, 2 * LR)
            both = product(vc[t], tile[pl.ds(at, 2 * LR), :], 1, 1)
            zs[t, d, 0] = both[:, :LR]
            zs[t, d, 1] = both[:, LR:]
            if d:
                cp = rcopy(
                    zs.at[t, d], zr.at[t, d - 1], rs_s.at[t, 6 + d], rs_r.at[t, 6 + d], (r, zcol(d))
                )
                cp.start()
                sends.append(cp)

        mirror(2)
        mirror(1)
        finish()
        mirror_on(2)
        direct(2)
        mirror_on(1)
        mirror(3)
        direct(1)
        mirror_on(3)
        direct(3)
        mirror(0)
        direct(0)
        mirror_on(0)
        own = product(value, diag[...], 1, 1)

        for d in (1, 3, 2):
            rcopy(mx.at[t, d], xr.at[t, d - 1], rs_s.at[t, 3 + d], rs_r.at[t, 3 + d], sib).wait_recv()
        ys[t] = (mx[t, 0, 1 - yh] + xr[t, 0, 1 - yh]) + (xr[t, 1, 1 - yh] + xr[t, 2, 1 - yh])
        cp_y = rcopy(ys.at[t], yr.at[t], rs_s.at[t, 10], rs_r.at[t, 10], yhp)
        cp_y.start()
        for d in (1, 3, 2):
            rcopy(zs.at[t, d], zr.at[t, d - 1], rs_s.at[t, 6 + d], rs_r.at[t, 6 + d], sib).wait_recv()
        ls[t] = (zs[t, 0, 1 - yl] + zr[t, 0, 1 - yl]) + (zr[t, 1, 1 - yl] + zr[t, 2, 1 - yl])
        cp_l = rcopy(ls.at[t], lr.at[t], rs_s.at[t, 11], rs_r.at[t, 11], ylp)
        cp_l.start()
        own += (mx[t, 0, yh] + xr[t, 0, yh]) + (xr[t, 1, yh] + xr[t, 2, yh])
        own += (zs[t, 0, yl] + zr[t, 0, yl]) + (zr[t, 1, yl] + zr[t, 2, yl])
        cp_y.wait_recv()
        own += yr[t]
        cp_l.wait_recv()
        own += lr[t]
        scale = jnp.where(t == 0, 1.0, 2.0).astype(F32)
        now = cur[...]
        following = scale * (own - centre * now) / halfwidth - prev[...]
        prev[...] = now
        cur[...] = following
        settle_sends(sends)
        cp_y.wait_send()
        cp_l.wait_send()
        return carry

    lax.fori_loop(0, DEG, degree, 0)
    y_out[...] = cur[...]
    rounded = cur[...].astype(BF16)
    out = (gram_out, ritz_out)

    def to_row(k):
        def step(j, carry):
            slab = pl.multiple_of(lax.rem(r + j, NR) * SLAB, SLAB)
            rcopy(
                part.at[k, pl.ds(slab, SLAB)], a1.at[k, j - 1], ar_s.at[k, 0, j], ar_r.at[k, 0, j],
                (lax.rem(r + j, NR), c),
            ).start()
            return carry

        lax.fori_loop(1, NR, step, 0)

    mine = pl.multiple_of(r * SLAB, SLAB)

    def to_col(k):
        def take(j, total):
            rcopy(
                a1.at[k, j - 1], a1.at[k, j - 1], ar_s.at[k, 0, j], ar_r.at[k, 0, j], sib
            ).wait_recv()
            return total + a1[k, j - 1]

        s2[k] = lax.fori_loop(1, NR, take, part[k, pl.ds(mine, SLAB), :])

        def step(j, carry):
            rcopy(
                s2.at[k], a2.at[k, j - 1], ar_s.at[k, 1, j], ar_r.at[k, 1, j],
                (r, lax.rem(c + j, NC)),
            ).start()
            return carry

        lax.fori_loop(1, NC, step, 0)

    def spread(k):
        def place(j, carry):
            rcopy(
                a2.at[k, j - 1], a2.at[k, j - 1], ar_s.at[k, 1, j], ar_r.at[k, 1, j], sib
            ).wait_recv()
            return carry

        lax.fori_loop(1, NC, place, 0)
        total = jnp.zeros((SLAB, K), F32)
        for i in range(NC):
            j = lax.rem(c - i + NC, NC)
            other = a2[k, jnp.maximum(j - 1, 0)]
            total = total + jnp.where(j == 0, s2[k], other)
        out[k][pl.ds(mine, SLAB), :] = total

        def step(j, carry):
            rcopy(
                out[k].at[pl.ds(mine, SLAB)], out[k].at[pl.ds(mine, SLAB)],
                ar_s.at[k, 2, j], ar_r.at[k, 2, j], (lax.rem(r + j, NR), c),
            ).start()
            return carry

        lax.fori_loop(1, NR, step, 0)

    def collect(k):
        def step(j, carry):
            there = pl.multiple_of(lax.rem(r - j + NR, NR) * SLAB, SLAB)
            rcopy(
                out[k].at[pl.ds(there, SLAB)], out[k].at[pl.ds(there, SLAB)],
                ar_s.at[k, 2, j], ar_r.at[k, 2, j], sib,
            ).wait_recv()
            return carry

        lax.fori_loop(1, NR, step, 0)

    def settle(k):
        def step(phase):
            def inner(j, carry):
                rcopy(
                    s2.at[k], s2.at[k], ar_s.at[k, phase, j], ar_r.at[k, phase, j], sib
                ).wait_send()
                return carry

            return inner

        lax.fori_loop(1, NR, step(0), 0)
        lax.fori_loop(1, NC, step(1), 0)
        lax.fori_loop(1, NR, step(2), 0)

    part[0] = product(rounded, rounded, 1, 1)
    to_row(0)
    sends, finish = gather(DEG, rounded)
    to_col(0)

    def three(rows, image):
        high = image.astype(BF16)
        rest = image - high.astype(F32)
        mid = rest.astype(BF16)
        low_part = (rest - mid.astype(F32)).astype(BF16)
        return product(rows, high, 1, 1) + (product(rows, mid, 1, 1) + product(rows, low_part, 1, 1))

    finish()
    part[1] = three(rounded, 0.5 * product(rounded, diag[...], 1, 1))
    for i in range(NC // 2):
        span = slice(i * 2 * LR, (i + 1) * 2 * LR)
        part[1] += three(vr[DEG, :, span], product(vc[DEG], tile[span, :], 1, 1))
    to_row(1)
    spread(0)
    to_col(1)
    collect(0)
    spread(1)
    collect(1)
    settle_sends(sends)
    settle(0)
    settle(1)


def dot_f32(a, b, left, right):
    return lax.dot_general(a, b, (((left,), (right,)), ((), ())), precision=HIGH, preferred_element_type=F32)


def dot_nn(a, b):
    return dot_f32(a, b, 1, 0)


def dot_nt(a, b):
    return dot_f32(a, b, 1, 1)


def dot_tn(a, b):
    return dot_f32(a, b, 0, 0)


def inverse_factor(block):
    rows = lax.broadcasted_iota(jnp.int32, (CB, 2 * CB), 0)
    lanes = lax.broadcasted_iota(jnp.int32, (CB, 2 * CB), 1)
    unit = jnp.where(lanes == rows + CB, 1.0, 0.0).astype(F32)
    x = jnp.where(lanes < CB, jnp.concatenate([block, block], axis=1), unit)
    for s in range(0, CB, STEP):
        col = [jnp.broadcast_to(x[:, s + j : s + j + 1], (CB, 2 * CB)) for j in range(STEP)]
        row = [x[s + j : s + j + 1, :] for j in range(STEP)]
        for j in range(STEP):
            d = col[j][s + j : s + j + 1, :]
            q = lax.rsqrt(d)
            col[j] = col[j] * q
            row[j] = row[j] * q
            for m in range(j + 1, STEP):
                f = col[j][s + m : s + m + 1, :]
                col[m] = col[m] - col[j] * f
                row[m] = row[m] - row[j] * f
        change = col[0] * row[0]
        for j in range(1, STEP):
            change = change + col[j] * row[j]
        x = jnp.where(rows >= s + STEP, x - change, x)
        for j in range(STEP):
            x = jnp.where(rows == s + j, row[j], x)
    return x[:, CB:]


def invert(a, b):
    b[...] = jnp.zeros_like(b)
    for k in range(0, K, CB):
        e = k + CB
        inv = inverse_factor(a[k:e, k:e])
        if k:
            b[k:e, :k] = dot_nn(inv, b[k:e, :k])
        b[k:e, k:e] = inv
        if e < K:
            u = dot_nn(inv, a[k:e, e:])
            a[e:, e:] = a[e:, e:] - dot_tn(u, u)
            b[e:, :e] = b[e:, :e] - dot_tn(u, b[k:e, :e])


def finish_kernel(cur, gram, half, orb, proj, a, b):
    scale = 1.0 / (NR * NC * LR)
    a[...] = gram[...] * scale
    invert(a, b)
    w = b[...]
    orb[...] = dot_f32(cur[...], w, 0, 1)
    s = half[...] * scale
    proj[...] = dot_nt(dot_nn(w, s) + dot_nt(w, s), w)


def local(orbitals_in, hblocks, block_cols, live_counts, onsite, cut_low, top_bound):
    vmem = pl.BlockSpec(memory_space=pltpu.VMEM)
    smem = pl.BlockSpec(memory_space=pltpu.SMEM)
    block = (K, LR)
    dma = pltpu.SemaphoreType.DMA
    current, gram_total, half_total = pl.pallas_call(
        kernel,
        out_shape=(
            jax.ShapeDtypeStruct(block, F32),
            jax.ShapeDtypeStruct((K, K), F32),
            jax.ShapeDtypeStruct((K, K), F32),
        ),
        in_specs=[pl.BlockSpec(memory_space=pl.ANY), vmem, vmem, vmem, vmem, smem, smem],
        out_specs=(vmem, vmem, vmem),
        scratch_shapes=[
            pltpu.VMEM((NC * LR, NR * LR), BF16),
            pltpu.VMEM(hblocks.shape, BF16),
            pltpu.VMEM((NR * 16, 32 * hblocks.shape[1]), F32),
            pltpu.VMEM((hblocks.shape[0], 32 * hblocks.shape[1]), F32),
            pltpu.VMEM((LR, LR), BF16),
            pltpu.VMEM((DEG + 1, K, NR * LR), BF16),
            pltpu.VMEM((DEG + 1, K, NC * LR), BF16),
            pltpu.VMEM((DEG, 4, 2, 2) + block, F32),
            pltpu.VMEM((DEG, 4, 2) + block, F32),
            pltpu.VMEM((DEG, 4, 2) + block, F32),
            pltpu.VMEM((DEG, 3, 2) + block, F32),
            pltpu.VMEM((DEG, 4, 2) + block, F32),
            pltpu.VMEM((DEG, 3, 2) + block, F32),
            pltpu.VMEM((DEG,) + block, F32),
            pltpu.VMEM((DEG,) + block, F32),
            pltpu.VMEM((DEG,) + block, F32),
            pltpu.VMEM((DEG,) + block, F32),
            pltpu.VMEM(block, F32),
            pltpu.VMEM(block, F32),
            pltpu.VMEM((2, K, K), F32),
            pltpu.VMEM((2, NR - 1, SLAB, K), F32),
            pltpu.VMEM((2, SLAB, K), F32),
            pltpu.VMEM((2, NC - 1, SLAB, K), F32),
            dma((DEG + 1, 22)),
            dma((DEG + 1, 22)),
            dma((DEG, 12)),
            dma((DEG, 12)),
            dma((2, 3, NR)),
            dma((2, 3, NR)),
            dma,
        ],
        compiler_params=pltpu.CompilerParams(
            collective_id=0, has_side_effects=True, vmem_limit_bytes=62 * 1024 * 1024
        ),
        name="filter_and_project",
    )(hblocks, block_cols, live_counts, orbitals_in, onsite.reshape(PB, BS, BS), cut_low, top_bound)
    return pl.pallas_call(
        finish_kernel,
        out_shape=(jax.ShapeDtypeStruct((LR, K), F32), jax.ShapeDtypeStruct((K, K), F32)),
        scratch_shapes=[pltpu.VMEM((K, K), F32)] * 2,
        name="orthonormalize",
    )(current, gram_total, half_total)


def solution(mesh):
    placed = (
        P(("row", "col"), None),
        P("row", "col", None),
        P("row", "col"),
        P("row", "col"),
        P(("row", "col"), None),
        P(),
        P(),
    )
    return jax.shard_map(
        local, mesh=mesh, in_specs=placed, out_specs=(P(("row", "col"), None), P()), check_vma=False
    )
```

```python
import jax
import jax.numpy as jnp
from jax import lax
from jax.experimental import pallas as pl
from jax.experimental.pallas import tpu as pltpu
from jax.sharding import PartitionSpec as P

BS = 64
K = 256
PB = 2
DEG = 3
LR = PB * BS
MESH = pl.DeviceIdType.MESH
F32 = jnp.float32
BF16 = jnp.bfloat16

NR = 16
NC = 8
SLAB = K // NR
HALF = 2
KH = K // HALF
CB = 64
STEP = 8
HIGH = lax.Precision.HIGHEST


def rcopy(src, dst, ssem, rsem, dev):
    return pltpu.make_async_remote_copy(
        src_ref=src, dst_ref=dst, send_sem=ssem, recv_sem=rsem, device_id=dev, device_id_type=MESH
    )


def product(a, b, left, right):
    return lax.dot_general(a, b, (((left,), (right,)), ((), ())), preferred_element_type=F32)


def build(blocks, cols, live, pick, tile):
    slots = lax.broadcasted_iota(jnp.int32, cols.shape, 1)
    wanted = jnp.where(slots < live[...], cols[...], -9).astype(F32).astype(BF16)
    count = cols.shape[1]
    depth = 4 * 8 * count
    lane = lax.broadcasted_iota(jnp.int32, (count, depth), 1)
    row = lax.broadcasted_iota(jnp.int32, (count, depth), 0)
    spread = jnp.where(lax.rem(lane, count) == row, 1.0, 0.0).astype(BF16)
    column = product(wanted, spread, 1, 0)
    column = column - lax.rem(lane // (8 * count), 2).astype(F32)

    high = lax.broadcasted_iota(jnp.int32, pick.shape, 0)
    deep = lax.broadcasted_iota(jnp.int32, pick.shape, 1)
    match = lax.rem(high, 16) == 2 * lax.rem(deep // count, 8) + deep // (16 * count)
    pick[...] = jnp.where(match, 2 * (high // 16), -99).astype(F32)
    first = lax.broadcasted_iota(jnp.int32, (8 * count, 2 * BS), 1) < BS
    none = jnp.zeros((8 * count, 2 * BS), BF16)
    return column, first, none


def build_row(i, blocks, column_ref, pick, first, none, tile):
    place = jnp.where(pick[...] == column_ref[pl.ds(i, 1), :], 1.0, 0.0).astype(BF16)
    for half in range(2):
        sides = []
        for p in (2 * half, 2 * half + 1):
            at = [(p * 8 + m) * 2 * BS for m in range(8)]
            plain = jnp.concatenate([blocks[i, :, a : a + 2 * BS] for a in at], axis=0)
            swapped = jnp.concatenate([plain[:, BS:], plain[:, :BS]], axis=1)
            sides.append(
                jnp.concatenate(
                    [
                        jnp.where(first, plain, none),
                        jnp.where(first, none, swapped),
                        jnp.where(first, swapped, none),
                        jnp.where(first, none, plain),
                    ],
                    axis=0,
                )
            )
        rows = product(place, jnp.concatenate(sides, axis=1), 1, 0).astype(BF16)
        for p in range(2):
            at = pl.multiple_of(i * BS + (2 * half + p) * 16, 16)
            for g in range(NR):
                tile[pl.ds(at, 16), g * LR : (g + 1) * LR] = rows[
                    g * 16 : (g + 1) * 16, p * LR : (p + 1) * LR
                ]


def dot_f32(a, b, left, right):
    return lax.dot_general(a, b, (((left,), (right,)), ((), ())), precision=HIGH, preferred_element_type=F32)


def dot_nn(a, b):
    return dot_f32(a, b, 1, 0)


def dot_nt(a, b):
    return dot_f32(a, b, 1, 1)


def dot_tn(a, b):
    return dot_f32(a, b, 0, 0)


def inverse_factor(block):
    rows = lax.broadcasted_iota(jnp.int32, (CB, 2 * CB), 0)
    lanes = lax.broadcasted_iota(jnp.int32, (CB, 2 * CB), 1)
    unit = jnp.where(lanes == rows + CB, 1.0, 0.0).astype(F32)
    x = jnp.where(lanes < CB, jnp.concatenate([block, block], axis=1), unit)
    for s in range(0, CB, STEP):
        col = [jnp.broadcast_to(x[:, s + j : s + j + 1], (CB, 2 * CB)) for j in range(STEP)]
        row = [x[s + j : s + j + 1, :] for j in range(STEP)]
        for j in range(STEP):
            d = col[j][s + j : s + j + 1, :]
            q = lax.rsqrt(d)
            col[j] = col[j] * q
            row[j] = row[j] * q
            for m in range(j + 1, STEP):
                f = col[j][s + m : s + m + 1, :]
                col[m] = col[m] - col[j] * f
                row[m] = row[m] - row[j] * f
        change = col[0] * row[0]
        for j in range(1, STEP):
            change = change + col[j] * row[j]
        x = jnp.where(rows >= s + STEP, x - change, x)
        for j in range(STEP):
            x = jnp.where(rows == s + j, row[j], x)
    return x[:, CB:]


def eliminate(a, b, block):
    k = block * CB
    e = k + CB
    inv = inverse_factor(a[k:e, k:e])
    if k:
        b[k:e, :k] = dot_nn(inv, b[k:e, :k])
    b[k:e, k:e] = inv
    if e < K:
        u = dot_nn(inv, a[k:e, e:])
        a[e:, e:] = a[e:, e:] - dot_tn(u, u)
        b[e:, :e] = b[e:, :e] - dot_tn(u, b[k:e, :e])


def kernel(
    hblocks, cols, live, y0, onsite, low, top, orb_out, proj_out,
    tile, blocks, pick, column, diag,
    vc, vr, ms, sr, mx, xr, zs, zr, ys, yr, ls, lr, prev, cur, part, a1, s2, a2, total, factor, inverse,
    ag_s, ag_r, rs_s, rs_r, ar_s, ar_r, load,
):
    fetch = pltpu.make_async_copy(hblocks, blocks, load)
    fetch.start()
    r = lax.axis_index("row")
    c = lax.axis_index("col")
    core = lax.rem(r, 2)
    x = lax.rem(r // 2, 4)
    yh = r // 8
    z = c // 2
    yl = lax.rem(c, 2)
    sib_r = r + 1 - 2 * core
    yhp_r = lax.rem(r + 8, NR)
    ylp_c = c + 1 - 2 * yl
    sib = (sib_r, c)
    yhp = (yhp_r, c)
    ylp = (r, ylp_c)

    def xrow(d, h=None, k=None):
        return (yh if h is None else h) * 8 + lax.rem(x + d + 4, 4) * 2 + (core if k is None else k)

    def zcol(d, l=None):
        return lax.rem(z + d + 4, 4) * 2 + (yl if l is None else l)

    def part_of(buf, t, u, slot):
        return buf.at[t, u, :, pl.ds(pl.multiple_of(slot * LR, LR), LR)]

    barrier = pltpu.get_barrier_semaphore()

    def greet_row(j, carry):
        pl.semaphore_signal(barrier, inc=1, device_id=(lax.rem(r + j, NR), c), device_id_type=MESH)
        return carry

    def greet_col(j, carry):
        pl.semaphore_signal(barrier, inc=1, device_id=(r, lax.rem(c + j, NC)), device_id_type=MESH)
        return carry

    lax.fori_loop(1, NR, greet_row, 0)
    lax.fori_loop(1, NC, greet_col, 0)

    cur[...] = y0[...].T
    prev[...] = jnp.zeros_like(prev)
    diag[...] = jnp.zeros_like(diag)
    for p in range(PB):
        diag[p * BS : (p + 1) * BS, p * BS : (p + 1) * BS] = onsite[p]
    pl.semaphore_wait(barrier, NR - 1 + NC - 1)


    def send_block(buf, t, u, slot, dev, k):
        side = 0 if buf is vc else 1
        rcopy(
            part_of(buf, t, u, slot), part_of(buf, t, u, slot),
            ag_s.at[t, u, side], ag_r.at[t, u, k], dev,
        ).start()

    def arrived(buf, t, u, slot, k):
        rcopy(
            part_of(buf, t, u, slot), part_of(buf, t, u, slot),
            ag_s.at[t, u, 0], ag_r.at[t, u, k], sib,
        ).wait_recv()

    def blocks_of(buf, t, u, count):
        return buf.at[t, u, :, pl.ds(0, count * LR)]

    def begin(t, u, value):
        vc[t, u, :, pl.ds(pl.multiple_of(r * LR, LR), LR)] = value
        vr[t, u, :, pl.ds(pl.multiple_of(c * LR, LR), LR)] = value
        send_block(vr, t, u, c, ylp, 5)
        send_block(vc, t, u, r, yhp, 1)
        for d in (2, 1, 3):
            send_block(vc, t, u, r, (xrow(d), c), 1 + d)
            send_block(vr, t, u, c, (r, zcol(d)), 6)
        send_block(vc, t, u, r, sib, 0)

    def relay(t, u):
        arrived(vr, t, u, ylp_c, 5)
        for d in (2, 1, 3):
            send_block(vr, t, u, ylp_c, (r, zcol(d)), 6)
        arrived(vc, t, u, yhp_r, 1)
        for d in (2, 1, 3):
            send_block(vc, t, u, yhp_r, (xrow(d), c), 6 + d)
        send_block(vc, t, u, yhp_r, sib, 0)

    def pass_on(t, u):
        for d in (1, 3, 2):
            arrived(vc, t, u, xrow(-d), 1 + d)
            send_block(vc, t, u, xrow(-d), sib, 0)
        for d in (1, 3, 2):
            arrived(vc, t, u, xrow(-d, h=1 - yh), 6 + d)
            send_block(vc, t, u, xrow(-d, h=1 - yh), sib, 0)
        six = blocks_of(vr, t, u, 6)
        rcopy(six, six, ag_s.at[t, u, 1], ag_r.at[t, u, 6], sib).wait_recv()

    def gathered(t, u):
        eight = blocks_of(vc, t, u, 8)
        rcopy(eight, eight, ag_s.at[t, u, 0], ag_r.at[t, u, 0], sib).wait_recv()

    def settle_gather(t, u):
        sent = blocks_of(vc, t, u, 15)
        rcopy(sent, sent, ag_s.at[t, u, 0], ag_r.at[t, u, 0], sib).wait_send()
        sent = blocks_of(vr, t, u, 7)
        rcopy(sent, sent, ag_s.at[t, u, 1], ag_r.at[t, u, 0], sib).wait_send()

    centre = 0.5 * (top[0] + low[0])
    halfwidth = 0.5 * (top[0] - low[0])

    def to_sib(t, u, d):
        return rcopy(
            ms.at[t, u, d, 1 - core], sr.at[t, u, d], rs_s.at[t, u, 0], rs_r.at[t, u, d], sib
        )

    def along_x(t, u, d):
        return rcopy(
            mx.at[t, u, d], xr.at[t, u, d - 1], rs_s.at[t, u, 1], rs_r.at[t, u, 4], (xrow(d), c)
        )

    def along_z(t, u, d):
        return rcopy(
            zs.at[t, u, d], zr.at[t, u, d - 1], rs_s.at[t, u, 2], rs_r.at[t, u, 5], (r, zcol(d))
        )

    def along_y(t, u):
        return (
            rcopy(ys.at[t, u], yr.at[t, u], rs_s.at[t, u, 3], rs_r.at[t, u, 6], yhp),
            rcopy(ls.at[t, u], lr.at[t, u], rs_s.at[t, u, 4], rs_r.at[t, u, 7], ylp),
        )

    def settle_reduce(t, u):
        rcopy(mx.at[t, u], mx.at[t, u], rs_s.at[t, u, 0], rs_r.at[t, u, 0], sib).wait_send()
        rcopy(xr.at[t, u], xr.at[t, u], rs_s.at[t, u, 1], rs_r.at[t, u, 4], sib).wait_send()
        rcopy(zr.at[t, u], zr.at[t, u], rs_s.at[t, u, 2], rs_r.at[t, u, 5], sib).wait_send()
        for cp in along_y(t, u):
            cp.wait_send()

    def products(t, u):
        def mirror(d):
            for h in range(2):
                at = pl.multiple_of(xrow(d, h=h, k=0) * LR, 2 * LR)
                both = product(vr[t, u], tile[:, pl.ds(at, 2 * LR)], 1, 0)
                ms[t, u, d, 0, h] = both[:, :LR]
                ms[t, u, d, 1, h] = both[:, LR:]
            to_sib(t, u, d).start()

        def mirror_on(d):
            to_sib(t, u, d).wait_recv()
            mx[t, u, d] = sr[t, u, d] + ms[t, u, d, core]
            if d:
                along_x(t, u, d).start()

        def direct(d):
            at = pl.multiple_of(zcol(d, l=0) * LR, 2 * LR)
            both = product(vc[t, u], tile[pl.ds(at, 2 * LR), :], 1, 1)
            zs[t, u, d, 0] = both[:, :LR]
            zs[t, u, d, 1] = both[:, LR:]
            if d:
                along_z(t, u, d).start()

        mirror(2)
        mirror(1)
        gathered(t, u)
        mirror_on(2)
        direct(2)
        mirror_on(1)
        mirror(3)
        direct(1)
        mirror_on(3)
        direct(3)
        mirror(0)
        direct(0)
        mirror_on(0)

    def summed(own, got, t, u, at):
        return (own[t, u, 0, at] + got[t, u, 0, at]) + (got[t, u, 1, at] + got[t, u, 2, at])

    def reduce(t, u):
        cp_y, cp_l = along_y(t, u)
        rcopy(xr.at[t, u], xr.at[t, u], rs_s.at[t, u, 1], rs_r.at[t, u, 4], sib).wait_recv()
        ys[t, u] = summed(mx, xr, t, u, 1 - yh)
        cp_y.start()
        rcopy(zr.at[t, u], zr.at[t, u], rs_s.at[t, u, 2], rs_r.at[t, u, 5], sib).wait_recv()
        ls[t, u] = summed(zs, zr, t, u, 1 - yl)
        cp_l.start()

    def update(t, u):
        span = slice(u * KH, (u + 1) * KH)
        cp_y, cp_l = along_y(t, u)
        now = cur[span, :]
        own = product(now.astype(BF16), diag[...], 1, 1)
        own += summed(mx, xr, t, u, yh)
        own += summed(zs, zr, t, u, yl)
        cp_y.wait_recv()
        own += yr[t, u]
        cp_l.wait_recv()
        own += lr[t, u]
        scale = jnp.where(t == 0, 1.0, 2.0).astype(F32)
        following = scale * (own - centre * now) / halfwidth - prev[span, :]
        prev[span, :] = now
        cur[span, :] = following
        begin(t + 1, u, following.astype(BF16))

    for u in range(HALF):
        begin(0, u, cur[u * KH : (u + 1) * KH, :].astype(BF16))

    def degree(t, carry):
        for u in range(HALF):
            relay(t, u)

        @pl.when(t == 0)
        def _():
            fetch.wait()
            spread, first, none = build(blocks, cols, live, pick, tile)
            column[...] = spread

            def one(i, inner):
                build_row(i, blocks, column, pick, first, none, tile)
                return inner

            lax.fori_loop(0, hblocks.shape[0], one, 0)

        @pl.when(t > 0)
        def _():
            for u in range(HALF):
                settle_gather(t - 1, u)
                settle_reduce(t - 1, u)

        for u in range(HALF):
            pass_on(t, u)
        for u in range(HALF):
            products(t, u)
        for u in range(HALF):
            reduce(t, u)
        for u in range(HALF):
            update(t, u)
        return carry

    lax.fori_loop(0, DEG, degree, 0)

    mine = pl.multiple_of(r * SLAB, SLAB)

    def to_row(k):
        def step(j, carry):
            slab = pl.multiple_of(lax.rem(r + j, NR) * SLAB, SLAB)
            rcopy(
                part.at[k, pl.ds(slab, SLAB)], a1.at[k, j - 1], ar_s.at[k, 0], ar_r.at[k, 0],
                (lax.rem(r + j, NR), c),
            ).start()
            return carry

        lax.fori_loop(1, NR, step, 0)

    def to_col(k):
        rcopy(a1.at[k], a1.at[k], ar_s.at[k, 0], ar_r.at[k, 0], sib).wait_recv()
        slab = part[k, pl.ds(mine, SLAB), :]
        for j in range(NR - 1):
            slab = slab + a1[k, j]
        a2[k, c] = slab
        s2[k] = slab

        def step(j, carry):
            rcopy(
                s2.at[k], a2.at[k, c], ar_s.at[k, 1], ar_r.at[k, 1], (r, lax.rem(c + j, NC))
            ).start()
            return carry

        lax.fori_loop(1, NC, step, 0)

    def spread_out(k):
        seven = a2.at[k, pl.ds(0, NC - 1)]
        rcopy(seven, seven, ar_s.at[k, 1], ar_r.at[k, 1], sib).wait_recv()
        slab = a2[k, 0]
        for j in range(1, NC):
            slab = slab + a2[k, j]
        total[k, pl.ds(mine, SLAB), :] = slab

        def step(j, carry):
            here = total.at[k, pl.ds(mine, SLAB)]
            rcopy(here, here, ar_s.at[k, 2], ar_r.at[k, 2], (lax.rem(r + j, NR), c)).start()
            return carry

        lax.fori_loop(1, NR, step, 0)

    def others(k):
        return total.at[k, pl.ds(0, K - SLAB)]

    def collect(k):
        rcopy(others(k), others(k), ar_s.at[k, 2], ar_r.at[k, 2], sib).wait_recv()

    def settle(k):
        rcopy(a1.at[k], a1.at[k], ar_s.at[k, 0], ar_r.at[k, 0], sib).wait_send()
        seven = a2.at[k, pl.ds(0, NC - 1)]
        rcopy(seven, seven, ar_s.at[k, 1], ar_r.at[k, 1], sib).wait_send()
        rcopy(others(k), others(k), ar_s.at[k, 2], ar_r.at[k, 2], sib).wait_send()

    def three(rows, image):
        high = image.astype(BF16)
        rest = image - high.astype(F32)
        mid = rest.astype(BF16)
        low_part = (rest - mid.astype(F32)).astype(BF16)
        return product(rows, high, 1, 1) + (product(rows, mid, 1, 1) + product(rows, low_part, 1, 1))

    rounded = cur[...].astype(BF16)
    part[0] = product(rounded, rounded, 1, 1)
    to_row(0)
    for u in range(HALF):
        relay(DEG, u)
    for u in range(HALF):
        pass_on(DEG, u)
    to_col(0)
    part[1] = three(rounded, 0.5 * product(rounded, diag[...], 1, 1))
    for u in range(HALF):
        gathered(DEG, u)
    for i in range(NC // 2):
        span = slice(i * 2 * LR, (i + 1) * 2 * LR)
        every = vc[DEG].reshape(K, NR * LR)
        image = product(every, tile[span, :], 1, 1)
        part[1] += three(vr[DEG, :, :, span].reshape(K, 2 * LR), image)
        if i == 1:
            spread_out(0)
    to_row(1)
    for u in range(HALF):
        settle_gather(DEG - 1, u)
        settle_reduce(DEG - 1, u)
        settle_gather(DEG, u)
    collect(0)
    scale = 1.0 / (NR * NC * LR)
    factor[...] = total[0] * scale
    inverse[...] = jnp.zeros_like(inverse)
    eliminate(factor, inverse, 0)
    eliminate(factor, inverse, 1)
    to_col(1)
    eliminate(factor, inverse, 2)
    spread_out(1)
    eliminate(factor, inverse, 3)
    w = inverse[...]
    orb_out[...] = dot_f32(cur[...], w, 0, 1)
    settle(0)
    collect(1)
    both = total[1] * scale
    proj_out[...] = dot_nt(dot_nn(w, both) + dot_nt(w, both), w)
    settle(1)


def local(orbitals_in, hblocks, block_cols, live_counts, onsite, cut_low, top_bound):
    vmem = pl.BlockSpec(memory_space=pltpu.VMEM)
    smem = pl.BlockSpec(memory_space=pltpu.SMEM)
    block = (KH, LR)
    steps = (DEG, HALF)
    dma = pltpu.SemaphoreType.DMA
    return pl.pallas_call(
        kernel,
        out_shape=(jax.ShapeDtypeStruct((LR, K), F32), jax.ShapeDtypeStruct((K, K), F32)),
        in_specs=[pl.BlockSpec(memory_space=pl.ANY), vmem, vmem, vmem, vmem, smem, smem],
        out_specs=(vmem, vmem),
        scratch_shapes=[
            pltpu.VMEM((NC * LR, NR * LR), BF16),
            pltpu.VMEM(hblocks.shape, BF16),
            pltpu.VMEM((NR * 16, 32 * hblocks.shape[1]), F32),
            pltpu.VMEM((hblocks.shape[0], 32 * hblocks.shape[1]), F32),
            pltpu.VMEM((LR, LR), BF16),
            pltpu.VMEM((DEG + 1, HALF, KH, NR * LR), BF16),
            pltpu.VMEM((DEG + 1, HALF, KH, NC * LR), BF16),
            pltpu.VMEM(steps + (4, 2, 2) + block, F32),
            pltpu.VMEM(steps + (4, 2) + block, F32),
            pltpu.VMEM(steps + (4, 2) + block, F32),
            pltpu.VMEM(steps + (3, 2) + block, F32),
            pltpu.VMEM(steps + (4, 2) + block, F32),
            pltpu.VMEM(steps + (3, 2) + block, F32),
            pltpu.VMEM(steps + block, F32),
            pltpu.VMEM(steps + block, F32),
            pltpu.VMEM(steps + block, F32),
            pltpu.VMEM(steps + block, F32),
            pltpu.VMEM((K, LR), F32),
            pltpu.VMEM((K, LR), F32),
            pltpu.VMEM((2, K, K), F32),
            pltpu.VMEM((2, NR - 1, SLAB, K), F32),
            pltpu.VMEM((2, SLAB, K), F32),
            pltpu.VMEM((2, NC, SLAB, K), F32),
            pltpu.VMEM((2, K, K), F32),
            pltpu.VMEM((K, K), F32),
            pltpu.VMEM((K, K), F32),
            dma((DEG + 1, HALF, 2)),
            dma((DEG + 1, HALF, 10)),
            dma((DEG, HALF, 5)),
            dma((DEG, HALF, 8)),
            dma((2, 3)),
            dma((2, 3)),
            dma,
        ],
        compiler_params=pltpu.CompilerParams(
            collective_id=0, has_side_effects=True, vmem_limit_bytes=62 * 1024 * 1024
        ),
        name="filter_and_project",
    )(hblocks, block_cols, live_counts, orbitals_in, onsite.reshape(PB, BS, BS), cut_low, top_bound)


def solution(mesh):
    placed = (
        P(("row", "col"), None),
        P("row", "col", None),
        P("row", "col"),
        P("row", "col"),
        P(("row", "col"), None),
        P(),
        P(),
    )
    return jax.shard_map(
        local, mesh=mesh, in_specs=placed, out_specs=(P(("row", "col"), None), P()), check_vma=False
    )
```

```python
import jax
import jax.numpy as jnp
from jax import lax
from jax.experimental import pallas as pl
from jax.experimental.pallas import tpu as pltpu
from jax.sharding import PartitionSpec as P

BS = 64
K = 256
PB = 2
DEG = 3
LR = PB * BS
MESH = pl.DeviceIdType.MESH
F32 = jnp.float32
BF16 = jnp.bfloat16

NR = 16
NC = 8
SLAB = K // NR
HALF = 1
KH = K // HALF
CB = 64
STEP = 8
HIGH = lax.Precision.HIGHEST


def rcopy(src, dst, ssem, rsem, dev):
    return pltpu.make_async_remote_copy(
        src_ref=src, dst_ref=dst, send_sem=ssem, recv_sem=rsem, device_id=dev, device_id_type=MESH
    )


def product(a, b, left, right):
    return lax.dot_general(a, b, (((left,), (right,)), ((), ())), preferred_element_type=F32)


def build(blocks, cols, live, pick, tile):
    slots = lax.broadcasted_iota(jnp.int32, cols.shape, 1)
    same = lax.broadcasted_iota(jnp.int32, cols.shape, 0) == slots
    counts = jnp.where(same, live[...].astype(F32), 0.0).sum(axis=1, keepdims=True)
    wanted = jnp.where(slots.astype(F32) < counts, cols[...].astype(F32), -9.0).astype(BF16)
    count = cols.shape[1]
    depth = 4 * 8 * count
    lane = lax.broadcasted_iota(jnp.int32, (count, depth), 1)
    row = lax.broadcasted_iota(jnp.int32, (count, depth), 0)
    spread = jnp.where(lax.rem(lane, count) == row, 1.0, 0.0).astype(BF16)
    column = product(wanted, spread, 1, 0)
    column = column - lax.rem(lane // (8 * count), 2).astype(F32)

    high = lax.broadcasted_iota(jnp.int32, pick.shape, 0)
    deep = lax.broadcasted_iota(jnp.int32, pick.shape, 1)
    match = lax.rem(high, 16) == 2 * lax.rem(deep // count, 8) + deep // (16 * count)
    pick[...] = jnp.where(match, 2 * (high // 16), -99).astype(F32)
    first = lax.broadcasted_iota(jnp.int32, (8 * count, 2 * BS), 1) < BS
    none = jnp.zeros((8 * count, 2 * BS), BF16)
    return column, first, none


def build_diag(onsite, diag):
    tiles = onsite[...].astype(F32)
    stack = jnp.concatenate(
        [tiles[:, m * 2 * BS : (m + 1) * 2 * BS] for m in range(BS // 2)], axis=0
    ).astype(BF16)
    row = lax.broadcasted_iota(jnp.int32, (BS, BS), 0)
    deep = lax.broadcasted_iota(jnp.int32, (BS, BS), 1)
    even = lax.rem(lax.broadcasted_iota(jnp.int32, (BS, 2 * BS), 0), 2) == 0
    left = lax.broadcasted_iota(jnp.int32, (BS, 2 * BS), 1) < BS
    for p in range(PB):
        pick = jnp.where(deep == row // 2 * PB + p, 1.0, 0.0).astype(BF16)
        plain = product(pick, stack, 1, 0)
        swapped = jnp.concatenate([plain[:, BS:], plain[:, :BS]], axis=1)
        rows = jnp.where(even, plain, swapped) if p == 0 else jnp.where(even, swapped, plain)
        rows = jnp.where(left, rows, 0.0) if p == 0 else jnp.where(left, 0.0, rows)
        diag[p * BS : (p + 1) * BS, :] = rows.astype(BF16)


def build_row(i, blocks, column_ref, pick, first, none, tile):
    place = jnp.where(pick[...] == column_ref[pl.ds(i, 1), :], 1.0, 0.0).astype(BF16)
    for half in range(2):
        sides = []
        for p in (2 * half, 2 * half + 1):
            at = [(p * 8 + m) * 2 * BS for m in range(8)]
            plain = jnp.concatenate([blocks[i, :, a : a + 2 * BS] for a in at], axis=0)
            swapped = jnp.concatenate([plain[:, BS:], plain[:, :BS]], axis=1)
            sides.append(
                jnp.concatenate(
                    [
                        jnp.where(first, plain, none),
                        jnp.where(first, none, swapped),
                        jnp.where(first, swapped, none),
                        jnp.where(first, none, plain),
                    ],
                    axis=0,
                )
            )
        rows = product(place, jnp.concatenate(sides, axis=1), 1, 0).astype(BF16)
        for p in range(2):
            at = pl.multiple_of(i * BS + (2 * half + p) * 16, 16)
            for g in range(NR):
                tile[pl.ds(at, 16), g * LR : (g + 1) * LR] = rows[
                    g * 16 : (g + 1) * 16, p * LR : (p + 1) * LR
                ]


def dot_f32(a, b, left, right):
    return lax.dot_general(a, b, (((left,), (right,)), ((), ())), precision=HIGH, preferred_element_type=F32)


def dot_nn(a, b):
    return dot_f32(a, b, 1, 0)


def dot_nt(a, b):
    return dot_f32(a, b, 1, 1)


def dot_tn(a, b):
    return dot_f32(a, b, 0, 0)


def inverse_factor(block):
    rows = lax.broadcasted_iota(jnp.int32, (CB, 2 * CB), 0)
    lanes = lax.broadcasted_iota(jnp.int32, (CB, 2 * CB), 1)
    unit = jnp.where(lanes == rows + CB, 1.0, 0.0).astype(F32)
    x = jnp.where(lanes < CB, jnp.concatenate([block, block], axis=1), unit)
    for s in range(0, CB, STEP):
        col = [jnp.broadcast_to(x[:, s + j : s + j + 1], (CB, 2 * CB)) for j in range(STEP)]
        row = [x[s + j : s + j + 1, :] for j in range(STEP)]
        for j in range(STEP):
            d = col[j][s + j : s + j + 1, :]
            q = lax.rsqrt(d)
            col[j] = col[j] * q
            row[j] = row[j] * q
            for m in range(j + 1, STEP):
                f = col[j][s + m : s + m + 1, :]
                col[m] = col[m] - col[j] * f
                row[m] = row[m] - row[j] * f
        change = col[0] * row[0]
        for j in range(1, STEP):
            change = change + col[j] * row[j]
        x = jnp.where(rows >= s + STEP, x - change, x)
        for j in range(STEP):
            x = jnp.where(rows == s + j, row[j], x)
    return x[:, CB:]


def eliminate(a, b, block):
    k = block * CB
    e = k + CB
    inv = inverse_factor(a[k:e, k:e])
    if k:
        b[k:e, :k] = dot_nn(inv, b[k:e, :k])
    b[k:e, k:e] = inv
    if e < K:
        u = dot_nn(inv, a[k:e, e:])
        a[e:, e:] = a[e:, e:] - dot_tn(u, u)
        b[e:, :e] = b[e:, :e] - dot_tn(u, b[k:e, :e])


def kernel(
    hblocks, cols, live, y0, onsite, low, top, orb_out, inv_out, ritz_out,
    tile, blocks, pick, column, diag,
    vc, vr, ms, sr, mx, xr, zs, zr, ys, yr, ls, lr, prev, cur, part, a1, s2, a2, total, factor, inverse,
    ag_s, ag_r, rs_s, rs_r, ar_s, ar_r, load,
):
    fetch = pltpu.make_async_copy(hblocks, blocks, load)
    fetch.start()
    r = lax.axis_index("row")
    c = lax.axis_index("col")
    core = lax.rem(r, 2)
    x = lax.rem(r // 2, 4)
    yh = r // 8
    z = c // 2
    yl = lax.rem(c, 2)
    sib_r = r + 1 - 2 * core
    yhp_r = lax.rem(r + 8, NR)
    ylp_c = c + 1 - 2 * yl
    sib = (sib_r, c)
    yhp = (yhp_r, c)
    ylp = (r, ylp_c)

    def xrow(d, h=None, k=None):
        return (yh if h is None else h) * 8 + lax.rem(x + d + 4, 4) * 2 + (core if k is None else k)

    def zcol(d, l=None):
        return lax.rem(z + d + 4, 4) * 2 + (yl if l is None else l)

    def part_of(buf, t, u, slot):
        return buf.at[t, u, :, pl.ds(pl.multiple_of(slot * LR, LR), LR)]

    barrier = pltpu.get_barrier_semaphore()

    def greet_row(j, carry):
        pl.semaphore_signal(barrier, inc=1, device_id=(lax.rem(r + j, NR), c), device_id_type=MESH)
        return carry

    def greet_col(j, carry):
        pl.semaphore_signal(barrier, inc=1, device_id=(r, lax.rem(c + j, NC)), device_id_type=MESH)
        return carry

    lax.fori_loop(1, NR, greet_row, 0)
    lax.fori_loop(1, NC, greet_col, 0)

    cur[...] = y0[...].T
    prev[...] = jnp.zeros_like(prev)
    build_diag(onsite, diag)
    fetch.wait()
    spread, first, none = build(blocks, cols, live, pick, tile)
    column[...] = spread

    def one(i, carry):
        build_row(i, blocks, column, pick, first, none, tile)
        return carry

    early = hblocks.shape[0] // 2
    lax.fori_loop(0, early, one, 0)
    pl.semaphore_wait(barrier, NR - 1 + NC - 1)


    def send_block(buf, t, u, slot, dev, k):
        side = 0 if buf is vc else 1
        rcopy(
            part_of(buf, t, u, slot), part_of(buf, t, u, slot),
            ag_s.at[t, u, side], ag_r.at[t, u, k], dev,
        ).start()

    def arrived(buf, t, u, slot, k):
        rcopy(
            part_of(buf, t, u, slot), part_of(buf, t, u, slot),
            ag_s.at[t, u, 0], ag_r.at[t, u, k], sib,
        ).wait_recv()

    def blocks_of(buf, t, u, count):
        return buf.at[t, u, :, pl.ds(0, count * LR)]

    def begin(t, u, value):
        vc[t, u, :, pl.ds(pl.multiple_of(r * LR, LR), LR)] = value
        vr[t, u, :, pl.ds(pl.multiple_of(c * LR, LR), LR)] = value
        send_block(vr, t, u, c, ylp, 5)
        send_block(vc, t, u, r, yhp, 1)
        for d in (2, 1, 3):
            send_block(vc, t, u, r, (xrow(d), c), 1 + d)
            send_block(vr, t, u, c, (r, zcol(d)), 6)
        send_block(vc, t, u, r, sib, 0)

    def relay(t, u):
        arrived(vr, t, u, ylp_c, 5)
        for d in (2, 1, 3):
            send_block(vr, t, u, ylp_c, (r, zcol(d)), 6)
        arrived(vc, t, u, yhp_r, 1)
        for d in (2, 1, 3):
            send_block(vc, t, u, yhp_r, (xrow(d), c), 6 + d)
        send_block(vc, t, u, yhp_r, sib, 0)

    def pass_on(t, u):
        for d in (1, 3, 2):
            arrived(vc, t, u, xrow(-d), 1 + d)
            send_block(vc, t, u, xrow(-d), sib, 0)
        for d in (1, 3, 2):
            arrived(vc, t, u, xrow(-d, h=1 - yh), 6 + d)
            send_block(vc, t, u, xrow(-d, h=1 - yh), sib, 0)
        six = blocks_of(vr, t, u, 6)
        rcopy(six, six, ag_s.at[t, u, 1], ag_r.at[t, u, 6], sib).wait_recv()

    def gathered(t, u):
        eight = blocks_of(vc, t, u, 8)
        rcopy(eight, eight, ag_s.at[t, u, 0], ag_r.at[t, u, 0], sib).wait_recv()

    def settle_gather(t, u):
        sent = blocks_of(vc, t, u, 15)
        rcopy(sent, sent, ag_s.at[t, u, 0], ag_r.at[t, u, 0], sib).wait_send()
        sent = blocks_of(vr, t, u, 7)
        rcopy(sent, sent, ag_s.at[t, u, 1], ag_r.at[t, u, 0], sib).wait_send()

    centre = 0.5 * (top[...] + low[...])
    halfwidth = 0.5 * (top[...] - low[...])


    def to_sib(t, u, e, d):
        return rcopy(
            ms.at[t, u, e, d, 1 - core], sr.at[t, u, e, d],
            rs_s.at[t, u, 0], rs_r.at[t, u, e * 4 + d], sib,
        )

    def along_x(t, u, e, d):
        return rcopy(
            mx.at[t, u, e, d], xr.at[t, u, e, d - 1],
            rs_s.at[t, u, 1], rs_r.at[t, u, 8 + e], (xrow(d), c),
        )

    def along_z(t, u, e, d):
        return rcopy(
            zs.at[t, u, e, d], zr.at[t, u, e, d - 1],
            rs_s.at[t, u, 2], rs_r.at[t, u, 10 + e], (r, zcol(d)),
        )

    def along_y(t, u):
        return (
            rcopy(ys.at[t, u], yr.at[t, u], rs_s.at[t, u, 3], rs_r.at[t, u, 12], yhp),
            rcopy(ls.at[t, u], lr.at[t, u], rs_s.at[t, u, 4], rs_r.at[t, u, 13], ylp),
        )

    def settle_reduce(t, u):
        rcopy(mx.at[t, u], mx.at[t, u], rs_s.at[t, u, 0], rs_r.at[t, u, 0], sib).wait_send()
        rcopy(xr.at[t, u], xr.at[t, u], rs_s.at[t, u, 1], rs_r.at[t, u, 4], sib).wait_send()
        rcopy(zr.at[t, u], zr.at[t, u], rs_s.at[t, u, 2], rs_r.at[t, u, 5], sib).wait_send()
        for cp in along_y(t, u):
            cp.wait_send()

    def products(t, u, e):
        def mirror(d):
            at = pl.multiple_of(xrow(d, h=yh if e == 0 else 1 - yh, k=0) * LR, 2 * LR)
            both = product(vr[t, u], tile[:, pl.ds(at, 2 * LR)], 1, 0)
            ms[t, u, e, d, 0] = both[:, :LR]
            ms[t, u, e, d, 1] = both[:, LR:]
            to_sib(t, u, e, d).start()

        def mirror_on(d):
            to_sib(t, u, e, d).wait_recv()
            mx[t, u, e, d] = sr[t, u, e, d] + ms[t, u, e, d, core]
            if d:
                along_x(t, u, e, d).start()

        def direct(d):
            if e:
                at = pl.multiple_of(zcol(d, l=0) * LR, 2 * LR)
                both = product(vc[t, u], tile[pl.ds(at, 2 * LR), :], 1, 1)
                zs[t, u, yl, d] = both[:, :LR]
                zs[t, u, 1 - yl, d] = both[:, LR:]
            if d:
                along_z(t, u, e, d).start()

        mirror(2)
        mirror(1)
        mirror(3)
        if e:
            gathered(t, u)
        direct(2)
        mirror_on(2)
        mirror_on(1)
        direct(1)
        mirror_on(3)
        direct(3)
        mirror(0)
        direct(0)
        mirror_on(0)

    def summed(own, got, t, u, e):
        return (own[t, u, e, 0] + got[t, u, e, 0]) + (got[t, u, e, 1] + got[t, u, e, 2])

    def arrived_x(t, u, e):
        all_x = xr.at[t, u, e]
        rcopy(all_x, all_x, rs_s.at[t, u, 1], rs_r.at[t, u, 8 + e], sib).wait_recv()

    def arrived_z(t, u, e):
        all_z = zr.at[t, u, e]
        rcopy(all_z, all_z, rs_s.at[t, u, 2], rs_r.at[t, u, 10 + e], sib).wait_recv()

    def reduce(t, u):
        cp_y, cp_l = along_y(t, u)
        arrived_x(t, u, 1)
        ys[t, u] = summed(mx, xr, t, u, 1)
        cp_y.start()
        arrived_z(t, u, 1)
        ls[t, u] = summed(zs, zr, t, u, 1)
        cp_l.start()

    def update(t, u):
        span = slice(u * KH, (u + 1) * KH)
        cp_y, cp_l = along_y(t, u)
        now = cur[span, :]
        own = product(now.astype(BF16), diag[...], 1, 1)
        arrived_x(t, u, 0)
        own += summed(mx, xr, t, u, 0)
        arrived_z(t, u, 0)
        own += summed(zs, zr, t, u, 0)
        cp_y.wait_recv()
        own += yr[t, u]
        cp_l.wait_recv()
        own += lr[t, u]
        scale = jnp.where(t == 0, 1.0, 2.0).astype(F32)
        following = scale * (own - centre * now) / halfwidth - prev[span, :]
        prev[span, :] = now
        cur[span, :] = following
        begin(t + 1, u, following.astype(BF16))

    for u in range(HALF):
        begin(0, u, cur[u * KH : (u + 1) * KH, :].astype(BF16))

    def degree(t, carry):
        for u in range(HALF):
            relay(t, u)

        @pl.when(t == 0)
        def _():
            lax.fori_loop(early, hblocks.shape[0], one, 0)

        @pl.when(t > 0)
        def _():
            for u in range(HALF):
                settle_gather(t - 1, u)
                settle_reduce(t - 1, u)

        for u in range(HALF):
            pass_on(t, u)
        for e in (1, 0):
            for u in range(HALF):
                products(t, u, e)
        for u in range(HALF):
            reduce(t, u)
        for u in range(HALF):
            update(t, u)
        return carry

    lax.fori_loop(0, DEG, degree, 0)

    mine = pl.multiple_of(r * SLAB, SLAB)

    def to_row(k):
        def step(j, carry):
            slab = pl.multiple_of(lax.rem(r + j, NR) * SLAB, SLAB)
            rcopy(
                part.at[k, pl.ds(slab, SLAB)], a1.at[k, j - 1], ar_s.at[k, 0], ar_r.at[k, 0],
                (lax.rem(r + j, NR), c),
            ).start()
            return carry

        lax.fori_loop(1, NR, step, 0)

    def to_col(k):
        rcopy(a1.at[k], a1.at[k], ar_s.at[k, 0], ar_r.at[k, 0], sib).wait_recv()
        slab = part[k, pl.ds(mine, SLAB), :]
        for j in range(NR - 1):
            slab = slab + a1[k, j]
        a2[k, c] = slab
        s2[k] = slab

        def step(j, carry):
            rcopy(
                s2.at[k], a2.at[k, c], ar_s.at[k, 1], ar_r.at[k, 1], (r, lax.rem(c + j, NC))
            ).start()
            return carry

        lax.fori_loop(1, NC, step, 0)

    def spread_out(k):
        seven = a2.at[k, pl.ds(0, NC - 1)]
        rcopy(seven, seven, ar_s.at[k, 1], ar_r.at[k, 1], sib).wait_recv()
        slab = a2[k, 0]
        for j in range(1, NC):
            slab = slab + a2[k, j]
        total[k, pl.ds(mine, SLAB), :] = slab

        def step(j, carry):
            here = total.at[k, pl.ds(mine, SLAB)]
            rcopy(here, here, ar_s.at[k, 2], ar_r.at[k, 2], (lax.rem(r + j, NR), c)).start()
            return carry

        lax.fori_loop(1, NR, step, 0)

    def others(k):
        return total.at[k, pl.ds(0, K - SLAB)]

    def collect(k):
        rcopy(others(k), others(k), ar_s.at[k, 2], ar_r.at[k, 2], sib).wait_recv()

    def settle(k):
        rcopy(a1.at[k], a1.at[k], ar_s.at[k, 0], ar_r.at[k, 0], sib).wait_send()
        seven = a2.at[k, pl.ds(0, NC - 1)]
        rcopy(seven, seven, ar_s.at[k, 1], ar_r.at[k, 1], sib).wait_send()
        rcopy(others(k), others(k), ar_s.at[k, 2], ar_r.at[k, 2], sib).wait_send()

    def three(rows, image):
        high = image.astype(BF16)
        rest = image - high.astype(F32)
        mid = rest.astype(BF16)
        low_part = (rest - mid.astype(F32)).astype(BF16)
        return product(rows, high, 1, 1) + (product(rows, mid, 1, 1) + product(rows, low_part, 1, 1))

    rounded = cur[...].astype(BF16)
    part[0] = product(rounded, rounded, 1, 1)
    to_row(0)
    for u in range(HALF):
        relay(DEG, u)
    for u in range(HALF):
        pass_on(DEG, u)
    to_col(0)
    part[1] = three(rounded, 0.5 * product(rounded, diag[...], 1, 1))
    for u in range(HALF):
        gathered(DEG, u)
    for i in range(NC // 2):
        span = slice(i * 2 * LR, (i + 1) * 2 * LR)
        every = vc[DEG].reshape(K, NR * LR)
        image = product(every, tile[span, :], 1, 1)
        part[1] += three(vr[DEG, :, :, span].reshape(K, 2 * LR), image)
    to_row(1)
    spread_out(0)
    for u in range(HALF):
        settle_gather(DEG - 1, u)
        settle_reduce(DEG - 1, u)
        settle_gather(DEG, u)
    scale = 1.0 / (NR * NC * LR)
    inverse[...] = jnp.zeros_like(inverse)
    to_col(1)
    collect(0)
    factor[...] = total[0] * scale
    eliminate(factor, inverse, 0)
    eliminate(factor, inverse, 1)
    spread_out(1)
    eliminate(factor, inverse, 2)
    eliminate(factor, inverse, 3)
    w = inverse[...]
    inv_out[...] = w
    orb_out[...] = dot_f32(cur[...], w, 0, 1)
    settle(0)
    collect(1)
    ritz_out[...] = total[1] * scale
    settle(1)


def project(made, inverse, half, orb, proj):
    w = inverse[...]
    both = half[...]
    orb[...] = made[...]
    proj[...] = dot_nt(dot_nn(w, both + both.T), w)


def local(orbitals_in, hblocks, block_cols, live_counts, onsite, cut_low, top_bound):
    vmem = pl.BlockSpec(memory_space=pltpu.VMEM)
    anywhere = pl.BlockSpec(memory_space=pl.ANY)
    block = (KH, LR)
    steps = (DEG, HALF)
    dma = pltpu.SemaphoreType.DMA
    square = jax.ShapeDtypeStruct((K, K), F32)
    rows = jax.ShapeDtypeStruct((LR, K), F32)
    orbitals, inverse, half = pl.pallas_call(
        kernel,
        out_shape=(rows, square, square),
        in_specs=[anywhere] + [vmem] * 6,
        out_specs=(vmem, vmem, vmem),
        scratch_shapes=[
            pltpu.VMEM((NC * LR, NR * LR), BF16),
            pltpu.VMEM(hblocks.shape, BF16),
            pltpu.VMEM((NR * 16, 32 * hblocks.shape[1]), F32),
            pltpu.VMEM((hblocks.shape[0], 32 * hblocks.shape[1]), F32),
            pltpu.VMEM((LR, LR), BF16),
            pltpu.VMEM((DEG + 1, HALF, KH, NR * LR), BF16),
            pltpu.VMEM((DEG + 1, HALF, KH, NC * LR), BF16),
            pltpu.VMEM(steps + (2, 4, 2) + block, F32),
            pltpu.VMEM(steps + (2, 4) + block, F32),
            pltpu.VMEM(steps + (2, 4) + block, F32),
            pltpu.VMEM(steps + (2, 3) + block, F32),
            pltpu.VMEM(steps + (2, 4) + block, F32),
            pltpu.VMEM(steps + (2, 3) + block, F32),
            pltpu.VMEM(steps + block, F32),
            pltpu.VMEM(steps + block, F32),
            pltpu.VMEM(steps + block, F32),
            pltpu.VMEM(steps + block, F32),
            pltpu.VMEM((K, LR), F32),
            pltpu.VMEM((K, LR), F32),
            pltpu.VMEM((2, K, K), F32),
            pltpu.VMEM((2, NR - 1, SLAB, K), F32),
            pltpu.VMEM((2, SLAB, K), F32),
            pltpu.VMEM((2, NC, SLAB, K), F32),
            pltpu.VMEM((2, K, K), F32),
            pltpu.VMEM((K, K), F32),
            pltpu.VMEM((K, K), F32),
            dma((DEG + 1, HALF, 2)),
            dma((DEG + 1, HALF, 10)),
            dma((DEG, HALF, 5)),
            dma((DEG, HALF, 14)),
            dma((2, 3)),
            dma((2, 3)),
            dma,
        ],
        compiler_params=pltpu.CompilerParams(
            collective_id=0, has_side_effects=True, vmem_limit_bytes=62 * 1024 * 1024
        ),
        name="filter_and_project",
    )(
        hblocks, block_cols, live_counts.reshape(1, -1), orbitals_in, onsite,
        cut_low, top_bound,
    )
    return pl.pallas_call(
        project,
        out_shape=(rows, square),
        name="project",
    )(orbitals, inverse, half)


def solution(mesh):
    placed = (
        P(("row", "col"), None),
        P("row", "col", None),
        P("row", "col"),
        P("row", "col"),
        P(("row", "col"), None),
        P(),
        P(),
    )
    return jax.shard_map(
        local, mesh=mesh, in_specs=placed, out_specs=(P(("row", "col"), None), P()), check_vma=False
    )
```

```python
import jax
import jax.numpy as jnp
from jax import lax
from jax.experimental import pallas as pl
from jax.experimental.pallas import tpu as pltpu
from jax.sharding import PartitionSpec as P

BS = 64
K = 256
PB = 2
DEG = 3
LR = PB * BS
MESH = pl.DeviceIdType.MESH
F32 = jnp.float32
BF16 = jnp.bfloat16

NR = 16
NC = 8
SLAB = K // NR
HALF = 1
KH = K // HALF
CB = 64
STEP = 8
HIGH = lax.Precision.HIGHEST


def rcopy(src, dst, ssem, rsem, dev):
    return pltpu.make_async_remote_copy(
        src_ref=src, dst_ref=dst, send_sem=ssem, recv_sem=rsem, device_id=dev, device_id_type=MESH
    )


def product(a, b, left, right):
    return lax.dot_general(a, b, (((left,), (right,)), ((), ())), preferred_element_type=F32)


def build(blocks, cols, live, pick, tile):
    slots = lax.broadcasted_iota(jnp.int32, cols.shape, 1)
    same = lax.broadcasted_iota(jnp.int32, cols.shape, 0) == slots
    counts = jnp.where(same, live[...].astype(F32), 0.0).sum(axis=1, keepdims=True)
    wanted = jnp.where(slots.astype(F32) < counts, cols[...].astype(F32), -9.0).astype(BF16)
    count = cols.shape[1]
    depth = 4 * 8 * count
    lane = lax.broadcasted_iota(jnp.int32, (count, depth), 1)
    row = lax.broadcasted_iota(jnp.int32, (count, depth), 0)
    spread = jnp.where(lax.rem(lane, count) == row, 1.0, 0.0).astype(BF16)
    column = product(wanted, spread, 1, 0)
    column = column - lax.rem(lane // (8 * count), 2).astype(F32)

    high = lax.broadcasted_iota(jnp.int32, pick.shape, 0)
    deep = lax.broadcasted_iota(jnp.int32, pick.shape, 1)
    match = lax.rem(high, 16) == 2 * lax.rem(deep // count, 8) + deep // (16 * count)
    pick[...] = jnp.where(match, 2 * (high // 16), -99).astype(F32)
    first = lax.broadcasted_iota(jnp.int32, (8 * count, 2 * BS), 1) < BS
    none = jnp.zeros((8 * count, 2 * BS), BF16)
    return column, first, none


def build_diag(onsite, diag):
    tiles = onsite[...].astype(F32)
    stack = jnp.concatenate(
        [tiles[:, m * 2 * BS : (m + 1) * 2 * BS] for m in range(BS // 2)], axis=0
    ).astype(BF16)
    row = lax.broadcasted_iota(jnp.int32, (BS, BS), 0)
    deep = lax.broadcasted_iota(jnp.int32, (BS, BS), 1)
    even = lax.rem(lax.broadcasted_iota(jnp.int32, (BS, 2 * BS), 0), 2) == 0
    left = lax.broadcasted_iota(jnp.int32, (BS, 2 * BS), 1) < BS
    for p in range(PB):
        pick = jnp.where(deep == row // 2 * PB + p, 1.0, 0.0).astype(BF16)
        plain = product(pick, stack, 1, 0)
        swapped = jnp.concatenate([plain[:, BS:], plain[:, :BS]], axis=1)
        rows = jnp.where(even, plain, swapped) if p == 0 else jnp.where(even, swapped, plain)
        rows = jnp.where(left, rows, 0.0) if p == 0 else jnp.where(left, 0.0, rows)
        diag[p * BS : (p + 1) * BS, :] = rows.astype(BF16)


def build_row(i, blocks, column_ref, pick, first, none, tile):
    place = jnp.where(pick[...] == column_ref[pl.ds(i, 1), :], 1.0, 0.0).astype(BF16)
    for half in range(2):
        sides = []
        for p in (2 * half, 2 * half + 1):
            at = [(p * 8 + m) * 2 * BS for m in range(8)]
            plain = jnp.concatenate([blocks[i, :, a : a + 2 * BS] for a in at], axis=0)
            swapped = jnp.concatenate([plain[:, BS:], plain[:, :BS]], axis=1)
            sides.append(
                jnp.concatenate(
                    [
                        jnp.where(first, plain, none),
                        jnp.where(first, none, swapped),
                        jnp.where(first, swapped, none),
                        jnp.where(first, none, plain),
                    ],
                    axis=0,
                )
            )
        rows = product(place, jnp.concatenate(sides, axis=1), 1, 0).astype(BF16)
        for p in range(2):
            at = pl.multiple_of(i * BS + (2 * half + p) * 16, 16)
            for g in range(NR):
                tile[pl.ds(at, 16), g * LR : (g + 1) * LR] = rows[
                    g * 16 : (g + 1) * 16, p * LR : (p + 1) * LR
                ]


def dot_f32(a, b, left, right):
    return lax.dot_general(a, b, (((left,), (right,)), ((), ())), precision=HIGH, preferred_element_type=F32)


def dot_nn(a, b):
    return dot_f32(a, b, 1, 0)


def dot_nt(a, b):
    return dot_f32(a, b, 1, 1)


def dot_tn(a, b):
    return dot_f32(a, b, 0, 0)


def inverse_factor(block):
    rows = lax.broadcasted_iota(jnp.int32, (CB, 2 * CB), 0)
    lanes = lax.broadcasted_iota(jnp.int32, (CB, 2 * CB), 1)
    unit = jnp.where(lanes == rows + CB, 1.0, 0.0).astype(F32)
    x = jnp.where(lanes < CB, jnp.concatenate([block, block], axis=1), unit)
    for s in range(0, CB, STEP):
        col = [jnp.broadcast_to(x[:, s + j : s + j + 1], (CB, 2 * CB)) for j in range(STEP)]
        row = [x[s + j : s + j + 1, :] for j in range(STEP)]
        for j in range(STEP):
            d = col[j][s + j : s + j + 1, :]
            q = lax.rsqrt(d)
            col[j] = col[j] * q
            row[j] = row[j] * q
            for m in range(j + 1, STEP):
                f = col[j][s + m : s + m + 1, :]
                col[m] = col[m] - col[j] * f
                row[m] = row[m] - row[j] * f
        change = col[0] * row[0]
        for j in range(1, STEP):
            change = change + col[j] * row[j]
        x = jnp.where(rows >= s + STEP, x - change, x)
        for j in range(STEP):
            x = jnp.where(rows == s + j, row[j], x)
    return x[:, CB:]


def eliminate(a, b, block):
    k = block * CB
    e = k + CB
    inv = inverse_factor(a[k:e, k:e])
    if k:
        b[k:e, :k] = dot_nn(inv, b[k:e, :k])
    b[k:e, k:e] = inv
    if e < K:
        u = dot_nn(inv, a[k:e, e:])
        a[e:, e:] = a[e:, e:] - dot_tn(u, u)
        b[e:, :e] = b[e:, :e] - dot_tn(u, b[k:e, :e])


def kernel(
    hblocks, cols, live, y0, onsite, low, top, orb_out, inv_out, ritz_out,
    tile, blocks, pick, column, diag,
    vc, vr, ms, sr, mx, xr, zs, zr, ys, yr, ls, lr, zf, prev, cur, part, a1, s2, a2, total, factor, inverse,
    ag_s, ag_r, rs_s, rs_r, ar_s, ar_r, load,
):
    fetch = pltpu.make_async_copy(hblocks, blocks, load)
    fetch.start()
    r = lax.axis_index("row")
    c = lax.axis_index("col")
    core = lax.rem(r, 2)
    x = lax.rem(r // 2, 4)
    yh = r // 8
    z = c // 2
    yl = lax.rem(c, 2)
    sib_r = r + 1 - 2 * core
    yhp_r = lax.rem(r + 8, NR)
    ylp_c = c + 1 - 2 * yl
    sib = (sib_r, c)
    yhp = (yhp_r, c)
    ylp = (r, ylp_c)

    def xrow(d, h=None, k=None):
        return (yh if h is None else h) * 8 + lax.rem(x + d + 4, 4) * 2 + (core if k is None else k)

    def zcol(d, l=None):
        return lax.rem(z + d + 4, 4) * 2 + (yl if l is None else l)

    def part_of(buf, t, u, slot):
        return buf.at[t, u, :, pl.ds(pl.multiple_of(slot * LR, LR), LR)]

    barrier = pltpu.get_barrier_semaphore()

    def greet_row(j, carry):
        pl.semaphore_signal(barrier, inc=1, device_id=(lax.rem(r + j, NR), c), device_id_type=MESH)
        return carry

    def greet_col(j, carry):
        pl.semaphore_signal(barrier, inc=1, device_id=(r, lax.rem(c + j, NC)), device_id_type=MESH)
        return carry

    lax.fori_loop(1, NR, greet_row, 0)
    lax.fori_loop(1, NC, greet_col, 0)

    cur[...] = y0[...].T
    prev[...] = jnp.zeros_like(prev)
    pl.semaphore_wait(barrier, NR - 1 + NC - 1)


    def send_block(buf, t, u, slot, dev, k):
        side = 0 if buf is vc else 1
        rcopy(
            part_of(buf, t, u, slot), part_of(buf, t, u, slot),
            ag_s.at[t, u, side], ag_r.at[t, u, k], dev,
        ).start()

    def arrived(buf, t, u, slot, k):
        rcopy(
            part_of(buf, t, u, slot), part_of(buf, t, u, slot),
            ag_s.at[t, u, 0], ag_r.at[t, u, k], sib,
        ).wait_recv()

    def blocks_of(buf, t, u, count):
        return buf.at[t, u, :, pl.ds(0, count * LR)]

    def begin(t, u, value):
        vc[t, u, :, pl.ds(pl.multiple_of(r * LR, LR), LR)] = value
        vr[t, u, :, pl.ds(pl.multiple_of(c * LR, LR), LR)] = value
        send_block(vr, t, u, c, ylp, 5)
        send_block(vc, t, u, r, yhp, 1)
        for d in (2, 1, 3):
            send_block(vc, t, u, r, (xrow(d), c), 1 + d)
            send_block(vr, t, u, c, (r, zcol(d)), 6)
        send_block(vc, t, u, r, sib, 0)

    def relay(t, u):
        arrived(vr, t, u, ylp_c, 5)
        for d in (2, 1, 3):
            send_block(vr, t, u, ylp_c, (r, zcol(d)), 6)
        arrived(vc, t, u, yhp_r, 1)
        for d in (2, 1, 3):
            send_block(vc, t, u, yhp_r, (xrow(d), c), 6 + d)
        send_block(vc, t, u, yhp_r, sib, 0)

    def pass_on(t, u):
        for d in (1, 3, 2):
            arrived(vc, t, u, xrow(-d), 1 + d)
            send_block(vc, t, u, xrow(-d), sib, 0)
        six = blocks_of(vr, t, u, 6)
        rcopy(six, six, ag_s.at[t, u, 1], ag_r.at[t, u, 6], sib).wait_recv()

    def pass_far(t, u):
        for d in (1, 3, 2):
            arrived(vc, t, u, xrow(-d, h=1 - yh), 6 + d)
            send_block(vc, t, u, xrow(-d, h=1 - yh), sib, 0)

    def gathered(t, u):
        eight = blocks_of(vc, t, u, 8)
        rcopy(eight, eight, ag_s.at[t, u, 0], ag_r.at[t, u, 0], sib).wait_recv()

    def settle_gather(t, u):
        sent = blocks_of(vc, t, u, 15)
        rcopy(sent, sent, ag_s.at[t, u, 0], ag_r.at[t, u, 0], sib).wait_send()
        sent = blocks_of(vr, t, u, 7)
        rcopy(sent, sent, ag_s.at[t, u, 1], ag_r.at[t, u, 0], sib).wait_send()

    centre = 0.5 * (top[...] + low[...])
    halfwidth = 0.5 * (top[...] - low[...])


    def to_sib(t, u, e, d):
        return rcopy(
            ms.at[t, u, e, d, 1 - core], sr.at[t, u, e, d],
            rs_s.at[t, u, 0], rs_r.at[t, u, e * 4 + d], sib,
        )

    def along_x(t, u, e, d):
        return rcopy(
            mx.at[t, u, e, d], xr.at[t, u, e, d - 1],
            rs_s.at[t, u, 1], rs_r.at[t, u, 8 + e], (xrow(d), c),
        )

    def along_z(t, u, e, d):
        return rcopy(
            zs.at[t, u, e, d], zr.at[t, u, e, d - 1],
            rs_s.at[t, u, 2 + 3 * e], rs_r.at[t, u, 10 + e], (r, zcol(d)),
        )

    def along_y(t, u):
        return (
            rcopy(ys.at[t, u], yr.at[t, u], rs_s.at[t, u, 3], rs_r.at[t, u, 12], yhp),
            rcopy(ls.at[t, u], lr.at[t, u], rs_s.at[t, u, 4], rs_r.at[t, u, 13], ylp),
        )

    def far_z(t, u):
        return rcopy(zs.at[t, u, 1, 2], zf.at[t, u], rs_s.at[t, u, 6], rs_r.at[t, u, 14], ylp)

    def settle_reduce(t, u):
        rcopy(mx.at[t, u], mx.at[t, u], rs_s.at[t, u, 0], rs_r.at[t, u, 0], sib).wait_send()
        rcopy(xr.at[t, u], xr.at[t, u], rs_s.at[t, u, 1], rs_r.at[t, u, 4], sib).wait_send()
        for e in range(2):
            sent = zr.at[t, u, e, pl.ds(0, 3 - e)]
            rcopy(sent, sent, rs_s.at[t, u, 2 + 3 * e], rs_r.at[t, u, 5], sib).wait_send()
        for cp in along_y(t, u) + (far_z(t, u),):
            cp.wait_send()

    def products(t, u, e):
        def mirror(d):
            at = pl.multiple_of(xrow(d, h=yh if e == 0 else 1 - yh, k=0) * LR, 2 * LR)
            both = product(vr[t, u], tile[:, pl.ds(at, 2 * LR)], 1, 0)
            ms[t, u, e, d, 0] = both[:, :LR]
            ms[t, u, e, d, 1] = both[:, LR:]
            to_sib(t, u, e, d).start()

        def mirror_on(d):
            to_sib(t, u, e, d).wait_recv()
            mx[t, u, e, d] = sr[t, u, e, d] + ms[t, u, e, d, core]
            if d:
                along_x(t, u, e, d).start()

        def direct(d):
            if e:
                at = pl.multiple_of(zcol(d, l=0) * LR, 2 * LR)
                both = product(vc[t, u], tile[pl.ds(at, 2 * LR), :], 1, 1)
                zs[t, u, yl, d] = both[:, :LR]
                zs[t, u, 1 - yl, d] = both[:, LR:]
            if d == 2 and e == 0:
                far_z(t, u).wait_recv()
                zs[t, u, 0, 2] = zs[t, u, 0, 2] + zf[t, u]
            if d == 2 and e == 1:
                far_z(t, u).start()
            elif d:
                along_z(t, u, e, d).start()

        if e:
            mirror(2)
            mirror(1)
            pass_far(t, u)
            mirror(3)
            for d in (2, 1, 3):
                mirror_on(d)
            gathered(t, u)
            for d in (2, 1, 3):
                direct(d)
            mirror(0)
            direct(0)
            mirror_on(0)
        else:
            for d in (1, 3, 2):
                mirror(d)
            for d in (1, 3):
                direct(d)
                mirror_on(d)
            mirror_on(2)
            mirror(0)
            direct(0)
            mirror_on(0)
            direct(2)

    def summed(own, got, t, u, e):
        return (own[t, u, e, 0] + got[t, u, e, 0]) + (got[t, u, e, 1] + got[t, u, e, 2])

    def arrived_x(t, u, e):
        all_x = xr.at[t, u, e]
        rcopy(all_x, all_x, rs_s.at[t, u, 1], rs_r.at[t, u, 8 + e], sib).wait_recv()

    def arrived_z(t, u, e):
        all_z = zr.at[t, u, e, pl.ds(0, 3 - e)]
        rcopy(all_z, all_z, rs_s.at[t, u, 2], rs_r.at[t, u, 10 + e], sib).wait_recv()

    def reduce(t, u):
        cp_y, cp_l = along_y(t, u)
        arrived_x(t, u, 1)
        ys[t, u] = summed(mx, xr, t, u, 1)
        cp_y.start()
        arrived_z(t, u, 1)
        ls[t, u] = (zs[t, u, 1, 0] + zr[t, u, 1, 0]) + zr[t, u, 1, 2]
        cp_l.start()

    def update(t, u):
        span = slice(u * KH, (u + 1) * KH)
        cp_y, cp_l = along_y(t, u)
        now = cur[span, :]
        own = product(now.astype(BF16), diag[...], 1, 1)
        arrived_x(t, u, 0)
        own += summed(mx, xr, t, u, 0)
        arrived_z(t, u, 0)
        own += summed(zs, zr, t, u, 0)
        cp_y.wait_recv()
        own += yr[t, u]
        cp_l.wait_recv()
        own += lr[t, u]
        scale = jnp.where(t == 0, 1.0, 2.0).astype(F32)
        following = scale * (own - centre * now) / halfwidth - prev[span, :]
        prev[span, :] = now
        cur[span, :] = following
        begin(t + 1, u, following.astype(BF16))

    for u in range(HALF):
        begin(0, u, cur[u * KH : (u + 1) * KH, :].astype(BF16))

    build_diag(onsite, diag)
    fetch.wait()
    spread, first, none = build(blocks, cols, live, pick, tile)
    column[...] = spread

    def one(i, carry):
        build_row(i, blocks, column, pick, first, none, tile)
        return carry

    early = hblocks.shape[0] // 2
    lax.fori_loop(0, early, one, 0)

    def degree(t, carry):
        for u in range(HALF):
            relay(t, u)

        @pl.when(t == 0)
        def _():
            lax.fori_loop(early, hblocks.shape[0], one, 0)

        @pl.when(t > 0)
        def _():
            for u in range(HALF):
                settle_gather(t - 1, u)
                settle_reduce(t - 1, u)

        for u in range(HALF):
            pass_on(t, u)
        for e in (1, 0):
            for u in range(HALF):
                products(t, u, e)
        for u in range(HALF):
            reduce(t, u)
        for u in range(HALF):
            update(t, u)
        return carry

    lax.fori_loop(0, DEG, degree, 0)

    mine = pl.multiple_of(r * SLAB, SLAB)

    def to_row(k):
        def step(j, carry):
            slab = pl.multiple_of(lax.rem(r + j, NR) * SLAB, SLAB)
            rcopy(
                part.at[k, pl.ds(slab, SLAB)], a1.at[k, j - 1], ar_s.at[k, 0], ar_r.at[k, 0],
                (lax.rem(r + j, NR), c),
            ).start()
            return carry

        lax.fori_loop(1, NR, step, 0)

    def to_col(k):
        rcopy(a1.at[k], a1.at[k], ar_s.at[k, 0], ar_r.at[k, 0], sib).wait_recv()
        slab = part[k, pl.ds(mine, SLAB), :]
        for j in range(NR - 1):
            slab = slab + a1[k, j]
        a2[k, c] = slab
        s2[k] = slab

        def step(j, carry):
            rcopy(
                s2.at[k], a2.at[k, c], ar_s.at[k, 1], ar_r.at[k, 1], (r, lax.rem(c + j, NC))
            ).start()
            return carry

        lax.fori_loop(1, NC, step, 0)

    def spread_out(k):
        seven = a2.at[k, pl.ds(0, NC - 1)]
        rcopy(seven, seven, ar_s.at[k, 1], ar_r.at[k, 1], sib).wait_recv()
        slab = a2[k, 0]
        for j in range(1, NC):
            slab = slab + a2[k, j]
        total[k, pl.ds(mine, SLAB), :] = slab

        def step(j, carry):
            here = total.at[k, pl.ds(mine, SLAB)]
            rcopy(here, here, ar_s.at[k, 2], ar_r.at[k, 2], (lax.rem(r + j, NR), c)).start()
            return carry

        lax.fori_loop(1, NR, step, 0)

    def others(k):
        return total.at[k, pl.ds(0, K - SLAB)]

    def collect(k):
        rcopy(others(k), others(k), ar_s.at[k, 2], ar_r.at[k, 2], sib).wait_recv()

    def settle(k):
        rcopy(a1.at[k], a1.at[k], ar_s.at[k, 0], ar_r.at[k, 0], sib).wait_send()
        seven = a2.at[k, pl.ds(0, NC - 1)]
        rcopy(seven, seven, ar_s.at[k, 1], ar_r.at[k, 1], sib).wait_send()
        rcopy(others(k), others(k), ar_s.at[k, 2], ar_r.at[k, 2], sib).wait_send()

    def three(rows, image):
        high = image.astype(BF16)
        rest = image - high.astype(F32)
        mid = rest.astype(BF16)
        low_part = (rest - mid.astype(F32)).astype(BF16)
        return product(rows, high, 1, 1) + (product(rows, mid, 1, 1) + product(rows, low_part, 1, 1))

    rounded = cur[...].astype(BF16)
    part[0] = product(rounded, rounded, 1, 1)
    to_row(0)
    for u in range(HALF):
        relay(DEG, u)
    for u in range(HALF):
        pass_on(DEG, u)
        pass_far(DEG, u)
    to_col(0)
    part[1] = three(rounded, 0.5 * product(rounded, diag[...], 1, 1))
    for u in range(HALF):
        gathered(DEG, u)
    for i in range(NC // 2):
        span = slice(i * 2 * LR, (i + 1) * 2 * LR)
        every = vc[DEG].reshape(K, NR * LR)
        image = product(every, tile[span, :], 1, 1)
        part[1] += three(vr[DEG, :, :, span].reshape(K, 2 * LR), image)
    to_row(1)
    spread_out(0)
    for u in range(HALF):
        settle_gather(DEG - 1, u)
        settle_reduce(DEG - 1, u)
        settle_gather(DEG, u)
    scale = 1.0 / (NR * NC * LR)
    inverse[...] = jnp.zeros_like(inverse)
    to_col(1)
    collect(0)
    factor[...] = total[0] * scale
    eliminate(factor, inverse, 0)
    eliminate(factor, inverse, 1)
    spread_out(1)
    eliminate(factor, inverse, 2)
    eliminate(factor, inverse, 3)
    w = inverse[...]
    inv_out[...] = w
    orb_out[...] = dot_f32(cur[...], w, 0, 1)
    settle(0)
    collect(1)
    ritz_out[...] = total[1] * scale
    settle(1)


def project(made, inverse, half, orb, proj):
    w = inverse[...]
    both = half[...]
    orb[...] = made[...]
    proj[...] = dot_nt(dot_nn(w, both + both.T), w)


def local(orbitals_in, hblocks, block_cols, live_counts, onsite, cut_low, top_bound):
    vmem = pl.BlockSpec(memory_space=pltpu.VMEM)
    anywhere = pl.BlockSpec(memory_space=pl.ANY)
    block = (KH, LR)
    steps = (DEG, HALF)
    dma = pltpu.SemaphoreType.DMA
    square = jax.ShapeDtypeStruct((K, K), F32)
    rows = jax.ShapeDtypeStruct((LR, K), F32)
    orbitals, inverse, half = pl.pallas_call(
        kernel,
        out_shape=(rows, square, square),
        in_specs=[anywhere] + [vmem] * 6,
        out_specs=(vmem, vmem, vmem),
        scratch_shapes=[
            pltpu.VMEM((NC * LR, NR * LR), BF16),
            pltpu.VMEM(hblocks.shape, BF16),
            pltpu.VMEM((NR * 16, 32 * hblocks.shape[1]), F32),
            pltpu.VMEM((hblocks.shape[0], 32 * hblocks.shape[1]), F32),
            pltpu.VMEM((LR, LR), BF16),
            pltpu.VMEM((DEG + 1, HALF, KH, NR * LR), BF16),
            pltpu.VMEM((DEG + 1, HALF, KH, NC * LR), BF16),
            pltpu.VMEM(steps + (2, 4, 2) + block, F32),
            pltpu.VMEM(steps + (2, 4) + block, F32),
            pltpu.VMEM(steps + (2, 4) + block, F32),
            pltpu.VMEM(steps + (2, 3) + block, F32),
            pltpu.VMEM(steps + (2, 4) + block, F32),
            pltpu.VMEM(steps + (2, 3) + block, F32),
            pltpu.VMEM(steps + block, F32),
            pltpu.VMEM(steps + block, F32),
            pltpu.VMEM(steps + block, F32),
            pltpu.VMEM(steps + block, F32),
            pltpu.VMEM(steps + block, F32),
            pltpu.VMEM((K, LR), F32),
            pltpu.VMEM((K, LR), F32),
            pltpu.VMEM((2, K, K), F32),
            pltpu.VMEM((2, NR - 1, SLAB, K), F32),
            pltpu.VMEM((2, SLAB, K), F32),
            pltpu.VMEM((2, NC, SLAB, K), F32),
            pltpu.VMEM((2, K, K), F32),
            pltpu.VMEM((K, K), F32),
            pltpu.VMEM((K, K), F32),
            dma((DEG + 1, HALF, 2)),
            dma((DEG + 1, HALF, 10)),
            dma((DEG, HALF, 7)),
            dma((DEG, HALF, 15)),
            dma((2, 3)),
            dma((2, 3)),
            dma,
        ],
        compiler_params=pltpu.CompilerParams(
            collective_id=0, has_side_effects=True, vmem_limit_bytes=62 * 1024 * 1024
        ),
        name="filter_and_project",
    )(
        hblocks, block_cols, live_counts.reshape(1, -1), orbitals_in, onsite,
        cut_low, top_bound,
    )
    return pl.pallas_call(
        project,
        out_shape=(rows, square),
        name="project",
    )(orbitals, inverse, half)


def solution(mesh):
    placed = (
        P(("row", "col"), None),
        P("row", "col", None),
        P("row", "col"),
        P("row", "col"),
        P(("row", "col"), None),
        P(),
        P(),
    )
    return jax.shard_map(
        local, mesh=mesh, in_specs=placed, out_specs=(P(("row", "col"), None), P()), check_vma=False
    )
```

```python
import jax
import jax.numpy as jnp
from jax import lax
from jax.experimental import pallas as pl
from jax.experimental.pallas import tpu as pltpu
from jax.sharding import PartitionSpec as P

BS = 64
K = 256
PB = 2
DEG = 3
LR = PB * BS
MESH = pl.DeviceIdType.MESH
F32 = jnp.float32
BF16 = jnp.bfloat16

NR = 16
NC = 8
SLAB = K // NR
HALF = 1
KH = K // HALF
CB = 64
STEP = 8
HIGH = lax.Precision.HIGHEST


def rcopy(src, dst, ssem, rsem, dev):
    return pltpu.make_async_remote_copy(
        src_ref=src, dst_ref=dst, send_sem=ssem, recv_sem=rsem, device_id=dev, device_id_type=MESH
    )


def product(a, b, left, right):
    return lax.dot_general(a, b, (((left,), (right,)), ((), ())), preferred_element_type=F32)


def build(blocks, cols, live, pick, tile):
    slots = lax.broadcasted_iota(jnp.int32, cols.shape, 1)
    same = lax.broadcasted_iota(jnp.int32, cols.shape, 0) == slots
    counts = jnp.where(same, live[...].astype(F32), 0.0).sum(axis=1, keepdims=True)
    wanted = jnp.where(slots.astype(F32) < counts, cols[...].astype(F32), -9.0).astype(BF16)
    count = cols.shape[1]
    depth = 4 * 8 * count
    lane = lax.broadcasted_iota(jnp.int32, (count, depth), 1)
    row = lax.broadcasted_iota(jnp.int32, (count, depth), 0)
    spread = jnp.where(lax.rem(lane, count) == row, 1.0, 0.0).astype(BF16)
    column = product(wanted, spread, 1, 0)
    column = column - lax.rem(lane // (8 * count), 2).astype(F32)

    high = lax.broadcasted_iota(jnp.int32, pick.shape, 0)
    deep = lax.broadcasted_iota(jnp.int32, pick.shape, 1)
    match = lax.rem(high, 16) == 2 * lax.rem(deep // count, 8) + deep // (16 * count)
    pick[...] = jnp.where(match, 2 * (high // 16), -99).astype(F32)
    first = lax.broadcasted_iota(jnp.int32, (8 * count, 2 * BS), 1) < BS
    none = jnp.zeros((8 * count, 2 * BS), BF16)
    return column, first, none


def build_diag(onsite, diag):
    tiles = onsite[...].astype(F32)
    stack = jnp.concatenate(
        [tiles[:, m * 2 * BS : (m + 1) * 2 * BS] for m in range(BS // 2)], axis=0
    ).astype(BF16)
    row = lax.broadcasted_iota(jnp.int32, (BS, BS), 0)
    deep = lax.broadcasted_iota(jnp.int32, (BS, BS), 1)
    even = lax.rem(lax.broadcasted_iota(jnp.int32, (BS, 2 * BS), 0), 2) == 0
    left = lax.broadcasted_iota(jnp.int32, (BS, 2 * BS), 1) < BS
    for p in range(PB):
        pick = jnp.where(deep == row // 2 * PB + p, 1.0, 0.0).astype(BF16)
        plain = product(pick, stack, 1, 0)
        swapped = jnp.concatenate([plain[:, BS:], plain[:, :BS]], axis=1)
        rows = jnp.where(even, plain, swapped) if p == 0 else jnp.where(even, swapped, plain)
        rows = jnp.where(left, rows, 0.0) if p == 0 else jnp.where(left, 0.0, rows)
        diag[p * BS : (p + 1) * BS, :] = rows.astype(BF16)


def build_row(i, blocks, column_ref, pick, first, none, tile):
    place = jnp.where(pick[...] == column_ref[pl.ds(i, 1), :], 1.0, 0.0).astype(BF16)
    for half in range(2):
        sides = []
        for p in (2 * half, 2 * half + 1):
            at = [(p * 8 + m) * 2 * BS for m in range(8)]
            plain = jnp.concatenate([blocks[i, :, a : a + 2 * BS] for a in at], axis=0)
            swapped = jnp.concatenate([plain[:, BS:], plain[:, :BS]], axis=1)
            sides.append(
                jnp.concatenate(
                    [
                        jnp.where(first, plain, none),
                        jnp.where(first, none, swapped),
                        jnp.where(first, swapped, none),
                        jnp.where(first, none, plain),
                    ],
                    axis=0,
                )
            )
        rows = product(place, jnp.concatenate(sides, axis=1), 1, 0).astype(BF16)
        for p in range(2):
            at = pl.multiple_of(i * BS + (2 * half + p) * 16, 16)
            for g in range(NR):
                tile[pl.ds(at, 16), g * LR : (g + 1) * LR] = rows[
                    g * 16 : (g + 1) * 16, p * LR : (p + 1) * LR
                ]


def dot_f32(a, b, left, right):
    return lax.dot_general(a, b, (((left,), (right,)), ((), ())), precision=HIGH, preferred_element_type=F32)


def dot_nn(a, b):
    return dot_f32(a, b, 1, 0)


def dot_nt(a, b):
    return dot_f32(a, b, 1, 1)


def dot_tn(a, b):
    return dot_f32(a, b, 0, 0)


def inverse_factor(block):
    rows = lax.broadcasted_iota(jnp.int32, (CB, 2 * CB), 0)
    lanes = lax.broadcasted_iota(jnp.int32, (CB, 2 * CB), 1)
    unit = jnp.where(lanes == rows + CB, 1.0, 0.0).astype(F32)
    x = jnp.where(lanes < CB, jnp.concatenate([block, block], axis=1), unit)
    for s in range(0, CB, STEP):
        col = [jnp.broadcast_to(x[:, s + j : s + j + 1], (CB, 2 * CB)) for j in range(STEP)]
        row = [x[s + j : s + j + 1, :] for j in range(STEP)]
        for j in range(STEP):
            d = col[j][s + j : s + j + 1, :]
            q = lax.rsqrt(d)
            col[j] = col[j] * q
            row[j] = row[j] * q
            for m in range(j + 1, STEP):
                f = col[j][s + m : s + m + 1, :]
                col[m] = col[m] - col[j] * f
                row[m] = row[m] - row[j] * f
        change = col[0] * row[0]
        for j in range(1, STEP):
            change = change + col[j] * row[j]
        x = jnp.where(rows >= s + STEP, x - change, x)
        for j in range(STEP):
            x = jnp.where(rows == s + j, row[j], x)
    return x[:, CB:]


def eliminate(a, b, block):
    k = block * CB
    e = k + CB
    inv = inverse_factor(a[k:e, k:e])
    if k:
        b[k:e, :k] = dot_nn(inv, b[k:e, :k])
    b[k:e, k:e] = inv
    if e < K:
        u = dot_nn(inv, a[k:e, e:])
        a[e:, e:] = a[e:, e:] - dot_tn(u, u)
        b[e:, :e] = b[e:, :e] - dot_tn(u, b[k:e, :e])


def kernel(
    hblocks, cols, live, y0, onsite, low, top, orb_out, inv_out, ritz_out,
    tile, blocks, pick, column, diag,
    vc, vr, ms, sr, mx, xr, zs, zr, ys, yr, ls, lr, zf, prev, cur, part, a1, s2, a2, total, factor, inverse,
    ag_s, ag_r, rs_s, rs_r, ar_s, ar_r, load,
):
    fetch = pltpu.make_async_copy(hblocks, blocks, load)
    fetch.start()
    r = lax.axis_index("row")
    c = lax.axis_index("col")
    core = lax.rem(r, 2)
    x = lax.rem(r // 2, 4)
    yh = r // 8
    z = c // 2
    yl = lax.rem(c, 2)
    sib_r = r + 1 - 2 * core
    yhp_r = lax.rem(r + 8, NR)
    ylp_c = c + 1 - 2 * yl
    sib = (sib_r, c)
    yhp = (yhp_r, c)
    ylp = (r, ylp_c)

    def xrow(d, h=None, k=None):
        return (yh if h is None else h) * 8 + lax.rem(x + d + 4, 4) * 2 + (core if k is None else k)

    def zcol(d, l=None):
        return lax.rem(z + d + 4, 4) * 2 + (yl if l is None else l)

    def part_of(buf, t, u, slot):
        return buf.at[t, u, :, pl.ds(pl.multiple_of(slot * LR, LR), LR)]

    upper = yh == 0
    lower = yh == 1
    yr[...] = jnp.zeros_like(yr)
    barrier = pltpu.get_barrier_semaphore()

    def greet_row(j, carry):
        pl.semaphore_signal(barrier, inc=1, device_id=(lax.rem(r + j, NR), c), device_id_type=MESH)
        return carry

    def greet_col(j, carry):
        pl.semaphore_signal(barrier, inc=1, device_id=(r, lax.rem(c + j, NC)), device_id_type=MESH)
        return carry

    lax.fori_loop(1, NR, greet_row, 0)
    lax.fori_loop(1, NC, greet_col, 0)

    cur[...] = y0[...].T
    prev[...] = jnp.zeros_like(prev)
    pl.semaphore_wait(barrier, NR - 1 + NC - 1)


    def send_block(buf, t, u, slot, dev, k):
        side = 0 if buf is vc else 1
        rcopy(
            part_of(buf, t, u, slot), part_of(buf, t, u, slot),
            ag_s.at[t, u, side], ag_r.at[t, u, k], dev,
        ).start()

    def arrived(buf, t, u, slot, k):
        rcopy(
            part_of(buf, t, u, slot), part_of(buf, t, u, slot),
            ag_s.at[t, u, 0], ag_r.at[t, u, k], sib,
        ).wait_recv()

    def blocks_of(buf, t, u, count):
        return buf.at[t, u, :, pl.ds(0, count * LR)]

    def begin(t, u, value):
        vc[t, u, :, pl.ds(pl.multiple_of(r * LR, LR), LR)] = value
        vr[t, u, :, pl.ds(pl.multiple_of(c * LR, LR), LR)] = value
        send_block(vr, t, u, c, ylp, 5)

        @pl.when(lower)
        def _():
            send_block(vc, t, u, r, yhp, 1)

        for d in (2, 1, 3):
            send_block(vc, t, u, r, (xrow(d), c), 1 + d)
            send_block(vr, t, u, c, (r, zcol(d)), 6)
        send_block(vc, t, u, r, sib, 0)

    def relay(t, u):
        arrived(vr, t, u, ylp_c, 5)
        for d in (2, 1, 3):
            send_block(vr, t, u, ylp_c, (r, zcol(d)), 6)

        @pl.when(upper)
        def _():
            arrived(vc, t, u, yhp_r, 1)
            for d in (2, 1, 3):
                send_block(vc, t, u, yhp_r, (xrow(d), c), 6 + d)
            send_block(vc, t, u, yhp_r, sib, 0)

    def pass_on(t, u):
        for d in (1, 3, 2):
            arrived(vc, t, u, xrow(-d), 1 + d)
            send_block(vc, t, u, xrow(-d), sib, 0)
        six = blocks_of(vr, t, u, 6)
        rcopy(six, six, ag_s.at[t, u, 1], ag_r.at[t, u, 6], sib).wait_recv()

    def pass_far(t, u):
        @pl.when(upper)
        def _():
            for d in (1, 3, 2):
                arrived(vc, t, u, xrow(-d, h=1 - yh), 6 + d)
                send_block(vc, t, u, xrow(-d, h=1 - yh), sib, 0)

    def wait_blocks(buf, t, u, count, side, received):
        some = blocks_of(buf, t, u, count)
        cp = rcopy(some, some, ag_s.at[t, u, side], ag_r.at[t, u, 0], sib)
        if received:
            cp.wait_recv()
        else:
            cp.wait_send()

    def gathered(t, u):
        pl.when(upper)(lambda: wait_blocks(vc, t, u, 8, 0, True))
        pl.when(lower)(lambda: wait_blocks(vc, t, u, 4, 0, True))

    def settle_gather(t, u):
        pl.when(upper)(lambda: wait_blocks(vc, t, u, 14, 0, False))
        pl.when(lower)(lambda: wait_blocks(vc, t, u, 8, 0, False))
        wait_blocks(vr, t, u, 7, 1, False)

    centre = 0.5 * (top[...] + low[...])
    halfwidth = 0.5 * (top[...] - low[...])


    def to_sib(t, u, e, d):
        return rcopy(
            ms.at[t, u, e, d, 1 - core], sr.at[t, u, e, d],
            rs_s.at[t, u, 0], rs_r.at[t, u, e * 4 + d], sib,
        )

    def along_x(t, u, e, d):
        return rcopy(
            mx.at[t, u, e, d], xr.at[t, u, e, d - 1],
            rs_s.at[t, u, 1], rs_r.at[t, u, 8 + e], (xrow(d), c),
        )

    def along_z(t, u, e, d):
        return rcopy(
            zs.at[t, u, e, d], zr.at[t, u, e, d - 1],
            rs_s.at[t, u, 2 + 3 * e], rs_r.at[t, u, 10 + e], (r, zcol(d)),
        )

    def along_y(t, u):
        return (
            rcopy(ys.at[t, u], yr.at[t, u], rs_s.at[t, u, 3], rs_r.at[t, u, 12], yhp),
            rcopy(ls.at[t, u], lr.at[t, u], rs_s.at[t, u, 4], rs_r.at[t, u, 13], ylp),
        )

    def far_z(t, u):
        return rcopy(zs.at[t, u, 1, 2], zf.at[t, u], rs_s.at[t, u, 6], rs_r.at[t, u, 14], ylp)

    def settle_reduce(t, u):
        def settle_x(own, got):
            rcopy(own, own, rs_s.at[t, u, 0], rs_r.at[t, u, 0], sib).wait_send()
            rcopy(got, got, rs_s.at[t, u, 1], rs_r.at[t, u, 4], sib).wait_send()

        @pl.when(upper)
        def _():
            settle_x(mx.at[t, u], xr.at[t, u])
            along_y(t, u)[0].wait_send()

        @pl.when(lower)
        def _():
            settle_x(mx.at[t, u, 0], xr.at[t, u, 0])

        for e in range(2):
            sent = zr.at[t, u, e, pl.ds(0, 3 - e)]
            rcopy(sent, sent, rs_s.at[t, u, 2 + 3 * e], rs_r.at[t, u, 5], sib).wait_send()
        for cp in (along_y(t, u)[1], far_z(t, u)):
            cp.wait_send()

    def products(t, u, e):
        def mirror(d):
            at = pl.multiple_of(xrow(d, h=yh if e == 0 else 1 - yh, k=0) * LR, 2 * LR)
            both = product(vr[t, u], tile[:, pl.ds(at, 2 * LR)], 1, 0)
            ms[t, u, e, d, 0] = both[:, :LR]
            ms[t, u, e, d, 1] = both[:, LR:]
            to_sib(t, u, e, d).start()

        def mirror_on(d):
            to_sib(t, u, e, d).wait_recv()
            mx[t, u, e, d] = sr[t, u, e, d] + ms[t, u, e, d, core]
            if d:
                along_x(t, u, e, d).start()

        def direct(d):
            if e:
                at = pl.multiple_of(zcol(d, l=0) * LR, 2 * LR)
                both = product(vc[t, u], tile[pl.ds(at, 2 * LR), :], 1, 1)
                zs[t, u, yl, d] = both[:, :LR]
                zs[t, u, 1 - yl, d] = both[:, LR:]
            if d == 2 and e == 0:
                far_z(t, u).wait_recv()
                zs[t, u, 0, 2] = zs[t, u, 0, 2] + zf[t, u]
            if d == 2 and e == 1:
                far_z(t, u).start()
            elif d:
                along_z(t, u, e, d).start()

        if e:
            @pl.when(upper)
            def _():
                mirror(2)
                mirror(1)

            pass_far(t, u)

            @pl.when(upper)
            def _():
                mirror(3)
                for d in (2, 1, 3):
                    mirror_on(d)

            gathered(t, u)
            for d in (2, 1, 3):
                direct(d)

            @pl.when(upper)
            def _():
                mirror(0)
                mirror_on(0)

            direct(0)
        else:
            for d in (1, 3, 2):
                mirror(d)
            for d in (1, 3):
                direct(d)
                mirror_on(d)
            mirror_on(2)
            mirror(0)
            direct(0)
            mirror_on(0)
            direct(2)

    def summed(own, got, t, u, e):
        return (own[t, u, e, 0] + got[t, u, e, 0]) + (got[t, u, e, 1] + got[t, u, e, 2])

    def arrived_x(t, u, e):
        all_x = xr.at[t, u, e]
        rcopy(all_x, all_x, rs_s.at[t, u, 1], rs_r.at[t, u, 8 + e], sib).wait_recv()

    def arrived_z(t, u, e):
        all_z = zr.at[t, u, e, pl.ds(0, 3 - e)]
        rcopy(all_z, all_z, rs_s.at[t, u, 2], rs_r.at[t, u, 10 + e], sib).wait_recv()

    def reduce(t, u):
        @pl.when(upper)
        def _():
            arrived_x(t, u, 1)
            ys[t, u] = summed(mx, xr, t, u, 1)
            along_y(t, u)[0].start()

        arrived_z(t, u, 1)
        ls[t, u] = (zs[t, u, 1, 0] + zr[t, u, 1, 0]) + zr[t, u, 1, 2]
        along_y(t, u)[1].start()

    def update(t, u):
        span = slice(u * KH, (u + 1) * KH)
        now = cur[span, :]
        own = product(now.astype(BF16), diag[...], 1, 1)
        arrived_x(t, u, 0)
        own += summed(mx, xr, t, u, 0)
        arrived_z(t, u, 0)
        own += summed(zs, zr, t, u, 0)
        pl.when(lower)(lambda: along_y(t, u)[0].wait_recv())
        own += yr[t, u]
        along_y(t, u)[1].wait_recv()
        own += lr[t, u]
        scale = jnp.where(t == 0, 1.0, 2.0).astype(F32)
        following = scale * (own - centre * now) / halfwidth - prev[span, :]
        prev[span, :] = now
        cur[span, :] = following
        begin(t + 1, u, following.astype(BF16))

    for u in range(HALF):
        begin(0, u, cur[u * KH : (u + 1) * KH, :].astype(BF16))

    @pl.when(lower)
    def _():
        vc[:, :, :, : NC * LR] = jnp.zeros((DEG + 1, HALF, KH, NC * LR), BF16)

    build_diag(onsite, diag)
    fetch.wait()
    spread, first, none = build(blocks, cols, live, pick, tile)
    column[...] = spread

    def one(i, carry):
        build_row(i, blocks, column, pick, first, none, tile)
        return carry

    early = hblocks.shape[0] // 2
    lax.fori_loop(0, early, one, 0)

    def degree(t, carry):
        for u in range(HALF):
            relay(t, u)

        @pl.when(t == 0)
        def _():
            lax.fori_loop(early, hblocks.shape[0], one, 0)

        @pl.when(t > 0)
        def _():
            for u in range(HALF):
                settle_gather(t - 1, u)
                settle_reduce(t - 1, u)

        for u in range(HALF):
            pass_on(t, u)
        for e in (1, 0):
            for u in range(HALF):
                products(t, u, e)
        for u in range(HALF):
            reduce(t, u)
        for u in range(HALF):
            update(t, u)
        return carry

    lax.fori_loop(0, DEG, degree, 0)

    mine = pl.multiple_of(r * SLAB, SLAB)

    def to_row(k):
        def step(j, carry):
            slab = pl.multiple_of(lax.rem(r + j, NR) * SLAB, SLAB)
            rcopy(
                part.at[k, pl.ds(slab, SLAB)], a1.at[k, j - 1], ar_s.at[k, 0], ar_r.at[k, 0],
                (lax.rem(r + j, NR), c),
            ).start()
            return carry

        lax.fori_loop(1, NR, step, 0)

    def to_col(k):
        rcopy(a1.at[k], a1.at[k], ar_s.at[k, 0], ar_r.at[k, 0], sib).wait_recv()
        slab = part[k, pl.ds(mine, SLAB), :]
        for j in range(NR - 1):
            slab = slab + a1[k, j]
        a2[k, c] = slab
        s2[k] = slab

        def step(j, carry):
            rcopy(
                s2.at[k], a2.at[k, c], ar_s.at[k, 1], ar_r.at[k, 1], (r, lax.rem(c + j, NC))
            ).start()
            return carry

        lax.fori_loop(1, NC, step, 0)

    def spread_out(k):
        seven = a2.at[k, pl.ds(0, NC - 1)]
        rcopy(seven, seven, ar_s.at[k, 1], ar_r.at[k, 1], sib).wait_recv()
        slab = a2[k, 0]
        for j in range(1, NC):
            slab = slab + a2[k, j]
        total[k, pl.ds(mine, SLAB), :] = slab

        def step(j, carry):
            here = total.at[k, pl.ds(mine, SLAB)]
            rcopy(here, here, ar_s.at[k, 2], ar_r.at[k, 2], (lax.rem(r + j, NR), c)).start()
            return carry

        lax.fori_loop(1, NR, step, 0)

    def others(k):
        return total.at[k, pl.ds(0, K - SLAB)]

    def collect(k):
        rcopy(others(k), others(k), ar_s.at[k, 2], ar_r.at[k, 2], sib).wait_recv()

    def settle(k):
        rcopy(a1.at[k], a1.at[k], ar_s.at[k, 0], ar_r.at[k, 0], sib).wait_send()
        seven = a2.at[k, pl.ds(0, NC - 1)]
        rcopy(seven, seven, ar_s.at[k, 1], ar_r.at[k, 1], sib).wait_send()
        rcopy(others(k), others(k), ar_s.at[k, 2], ar_r.at[k, 2], sib).wait_send()

    def three(rows, image):
        high = image.astype(BF16)
        rest = image - high.astype(F32)
        mid = rest.astype(BF16)
        low_part = (rest - mid.astype(F32)).astype(BF16)
        return product(rows, high, 1, 1) + (product(rows, mid, 1, 1) + product(rows, low_part, 1, 1))

    rounded = cur[...].astype(BF16)
    part[0] = product(rounded, rounded, 1, 1)
    to_row(0)
    for u in range(HALF):
        relay(DEG, u)
    for u in range(HALF):
        pass_on(DEG, u)
        pass_far(DEG, u)
    to_col(0)
    part[1] = three(rounded, 0.5 * product(rounded, diag[...], 1, 1))
    for u in range(HALF):
        gathered(DEG, u)
    for i in range(NC // 2):
        span = slice(i * 2 * LR, (i + 1) * 2 * LR)
        every = vc[DEG].reshape(K, NR * LR)
        image = product(every, tile[span, :], 1, 1)
        part[1] += three(vr[DEG, :, :, span].reshape(K, 2 * LR), image)
    to_row(1)
    spread_out(0)
    for u in range(HALF):
        settle_gather(DEG - 1, u)
        settle_reduce(DEG - 1, u)
        settle_gather(DEG, u)
    scale = 1.0 / (NR * NC * LR)
    inverse[...] = jnp.zeros_like(inverse)
    to_col(1)
    collect(0)
    factor[...] = total[0] * scale
    eliminate(factor, inverse, 0)
    eliminate(factor, inverse, 1)
    spread_out(1)
    eliminate(factor, inverse, 2)
    eliminate(factor, inverse, 3)
    w = inverse[...]
    inv_out[...] = w
    orb_out[...] = dot_f32(cur[...], w, 0, 1)
    settle(0)
    collect(1)
    ritz_out[...] = total[1] * scale
    settle(1)


def project(made, inverse, half, orb, proj):
    w = inverse[...]
    both = half[...]
    orb[...] = made[...]
    proj[...] = dot_nt(dot_nn(w, both + both.T), w)


def local(orbitals_in, hblocks, block_cols, live_counts, onsite, cut_low, top_bound):
    vmem = pl.BlockSpec(memory_space=pltpu.VMEM)
    anywhere = pl.BlockSpec(memory_space=pl.ANY)
    block = (KH, LR)
    steps = (DEG, HALF)
    dma = pltpu.SemaphoreType.DMA
    square = jax.ShapeDtypeStruct((K, K), F32)
    rows = jax.ShapeDtypeStruct((LR, K), F32)
    orbitals, inverse, half = pl.pallas_call(
        kernel,
        out_shape=(rows, square, square),
        in_specs=[anywhere] + [vmem] * 6,
        out_specs=(vmem, vmem, vmem),
        scratch_shapes=[
            pltpu.VMEM((NC * LR, NR * LR), BF16),
            pltpu.VMEM(hblocks.shape, BF16),
            pltpu.VMEM((NR * 16, 32 * hblocks.shape[1]), F32),
            pltpu.VMEM((hblocks.shape[0], 32 * hblocks.shape[1]), F32),
            pltpu.VMEM((LR, LR), BF16),
            pltpu.VMEM((DEG + 1, HALF, KH, NR * LR), BF16),
            pltpu.VMEM((DEG + 1, HALF, KH, NC * LR), BF16),
            pltpu.VMEM(steps + (2, 4, 2) + block, F32),
            pltpu.VMEM(steps + (2, 4) + block, F32),
            pltpu.VMEM(steps + (2, 4) + block, F32),
            pltpu.VMEM(steps + (2, 3) + block, F32),
            pltpu.VMEM(steps + (2, 4) + block, F32),
            pltpu.VMEM(steps + (2, 3) + block, F32),
            pltpu.VMEM(steps + block, F32),
            pltpu.VMEM(steps + block, F32),
            pltpu.VMEM(steps + block, F32),
            pltpu.VMEM(steps + block, F32),
            pltpu.VMEM(steps + block, F32),
            pltpu.VMEM((K, LR), F32),
            pltpu.VMEM((K, LR), F32),
            pltpu.VMEM((2, K, K), F32),
            pltpu.VMEM((2, NR - 1, SLAB, K), F32),
            pltpu.VMEM((2, SLAB, K), F32),
            pltpu.VMEM((2, NC, SLAB, K), F32),
            pltpu.VMEM((2, K, K), F32),
            pltpu.VMEM((K, K), F32),
            pltpu.VMEM((K, K), F32),
            dma((DEG + 1, HALF, 2)),
            dma((DEG + 1, HALF, 10)),
            dma((DEG, HALF, 7)),
            dma((DEG, HALF, 15)),
            dma((2, 3)),
            dma((2, 3)),
            dma,
        ],
        compiler_params=pltpu.CompilerParams(
            collective_id=0, has_side_effects=True, vmem_limit_bytes=62 * 1024 * 1024
        ),
        name="filter_and_project",
    )(
        hblocks, block_cols, live_counts.reshape(1, -1), orbitals_in, onsite,
        cut_low, top_bound,
    )
    return pl.pallas_call(
        project,
        out_shape=(rows, square),
        name="project",
    )(orbitals, inverse, half)


def solution(mesh):
    placed = (
        P(("row", "col"), None),
        P("row", "col", None),
        P("row", "col"),
        P("row", "col"),
        P(("row", "col"), None),
        P(),
        P(),
    )
    return jax.shard_map(
        local, mesh=mesh, in_specs=placed, out_specs=(P(("row", "col"), None), P()), check_vma=False
    )
```

```python
import jax
import jax.numpy as jnp
from jax import lax
from jax.experimental import pallas as pl
from jax.experimental.pallas import tpu as pltpu
from jax.sharding import PartitionSpec as P

BS = 64
K = 256
PB = 2
DEG = 3
LR = PB * BS
MESH = pl.DeviceIdType.MESH
F32 = jnp.float32
BF16 = jnp.bfloat16

NR = 16
NC = 8
SLAB = K // NR
HALF = 1
KH = K // HALF
CB = 64
STEP = 8
HIGH = lax.Precision.HIGHEST


def rcopy(src, dst, ssem, rsem, dev):
    return pltpu.make_async_remote_copy(
        src_ref=src, dst_ref=dst, send_sem=ssem, recv_sem=rsem, device_id=dev, device_id_type=MESH
    )


def product(a, b, left, right):
    return lax.dot_general(a, b, (((left,), (right,)), ((), ())), preferred_element_type=F32)


def build(blocks, cols, live, pick, tile):
    slots = lax.broadcasted_iota(jnp.int32, cols.shape, 1)
    same = lax.broadcasted_iota(jnp.int32, cols.shape, 0) == slots
    counts = jnp.where(same, live[...].astype(F32), 0.0).sum(axis=1, keepdims=True)
    wanted = jnp.where(slots.astype(F32) < counts, cols[...].astype(F32), -9.0).astype(BF16)
    count = cols.shape[1]
    depth = 4 * 8 * count
    lane = lax.broadcasted_iota(jnp.int32, (count, depth), 1)
    row = lax.broadcasted_iota(jnp.int32, (count, depth), 0)
    spread = jnp.where(lax.rem(lane, count) == row, 1.0, 0.0).astype(BF16)
    column = product(wanted, spread, 1, 0)
    column = column - lax.rem(lane // (8 * count), 2).astype(F32)

    high = lax.broadcasted_iota(jnp.int32, pick.shape, 0)
    deep = lax.broadcasted_iota(jnp.int32, pick.shape, 1)
    match = lax.rem(high, 16) == 2 * lax.rem(deep // count, 8) + deep // (16 * count)
    pick[...] = jnp.where(match, 2 * (high // 16), -99).astype(F32)
    first = lax.broadcasted_iota(jnp.int32, (8 * count, 2 * BS), 1) < BS
    none = jnp.zeros((8 * count, 2 * BS), BF16)
    return column, first, none


def build_diag(onsite, diag):
    tiles = onsite[...].astype(F32)
    stack = jnp.concatenate(
        [tiles[:, m * 2 * BS : (m + 1) * 2 * BS] for m in range(BS // 2)], axis=0
    ).astype(BF16)
    row = lax.broadcasted_iota(jnp.int32, (BS, BS), 0)
    deep = lax.broadcasted_iota(jnp.int32, (BS, BS), 1)
    even = lax.rem(lax.broadcasted_iota(jnp.int32, (BS, 2 * BS), 0), 2) == 0
    left = lax.broadcasted_iota(jnp.int32, (BS, 2 * BS), 1) < BS
    for p in range(PB):
        pick = jnp.where(deep == row // 2 * PB + p, 1.0, 0.0).astype(BF16)
        plain = product(pick, stack, 1, 0)
        swapped = jnp.concatenate([plain[:, BS:], plain[:, :BS]], axis=1)
        rows = jnp.where(even, plain, swapped) if p == 0 else jnp.where(even, swapped, plain)
        rows = jnp.where(left, rows, 0.0) if p == 0 else jnp.where(left, 0.0, rows)
        diag[p * BS : (p + 1) * BS, :] = rows.astype(BF16)


def build_row(i, blocks, column_ref, pick, first, none, tile):
    place = jnp.where(pick[...] == column_ref[pl.ds(i, 1), :], 1.0, 0.0).astype(BF16)
    for half in range(2):
        sides = []
        for p in (2 * half, 2 * half + 1):
            at = [(p * 8 + m) * 2 * BS for m in range(8)]
            plain = jnp.concatenate([blocks[i, :, a : a + 2 * BS] for a in at], axis=0)
            swapped = jnp.concatenate([plain[:, BS:], plain[:, :BS]], axis=1)
            sides.append(
                jnp.concatenate(
                    [
                        jnp.where(first, plain, none),
                        jnp.where(first, none, swapped),
                        jnp.where(first, swapped, none),
                        jnp.where(first, none, plain),
                    ],
                    axis=0,
                )
            )
        rows = product(place, jnp.concatenate(sides, axis=1), 1, 0).astype(BF16)
        for p in range(2):
            at = pl.multiple_of(i * BS + (2 * half + p) * 16, 16)
            for g in range(NR):
                tile[pl.ds(at, 16), g * LR : (g + 1) * LR] = rows[
                    g * 16 : (g + 1) * 16, p * LR : (p + 1) * LR
                ]


def dot_f32(a, b, left, right):
    return lax.dot_general(a, b, (((left,), (right,)), ((), ())), precision=HIGH, preferred_element_type=F32)


def dot_nn(a, b):
    return dot_f32(a, b, 1, 0)


def dot_nt(a, b):
    return dot_f32(a, b, 1, 1)


def dot_tn(a, b):
    return dot_f32(a, b, 0, 0)


def inverse_factor(block):
    rows = lax.broadcasted_iota(jnp.int32, (CB, 2 * CB), 0)
    lanes = lax.broadcasted_iota(jnp.int32, (CB, 2 * CB), 1)
    unit = jnp.where(lanes == rows + CB, 1.0, 0.0).astype(F32)
    x = jnp.where(lanes < CB, jnp.concatenate([block, block], axis=1), unit)
    for s in range(0, CB, STEP):
        col = [jnp.broadcast_to(x[:, s + j : s + j + 1], (CB, 2 * CB)) for j in range(STEP)]
        row = [x[s + j : s + j + 1, :] for j in range(STEP)]
        for j in range(STEP):
            d = col[j][s + j : s + j + 1, :]
            q = lax.rsqrt(d)
            col[j] = col[j] * q
            row[j] = row[j] * q
            for m in range(j + 1, STEP):
                f = col[j][s + m : s + m + 1, :]
                col[m] = col[m] - col[j] * f
                row[m] = row[m] - row[j] * f
        change = col[0] * row[0]
        for j in range(1, STEP):
            change = change + col[j] * row[j]
        x = jnp.where(rows >= s + STEP, x - change, x)
        for j in range(STEP):
            x = jnp.where(rows == s + j, row[j], x)
    return x[:, CB:]


def eliminate(a, b, block):
    k = block * CB
    e = k + CB
    inv = inverse_factor(a[k:e, k:e])
    if k:
        b[k:e, :k] = dot_nn(inv, b[k:e, :k])
    b[k:e, k:e] = inv
    if e < K:
        u = dot_nn(inv, a[k:e, e:])
        a[e:, e:] = a[e:, e:] - dot_tn(u, u)
        b[e:, :e] = b[e:, :e] - dot_tn(u, b[k:e, :e])


def kernel(
    hblocks, cols, live, y0, onsite, low, top, orb_out, inv_out, ritz_out,
    tile, blocks, pick, column, diag,
    vc, vr, ms, sr, mx, xr, zs, zr, ys, yr, ls, lr, zf, prev, cur, part, a1, s2, a2, total, factor, inverse,
    ag_s, ag_r, rs_s, rs_r, ar_s, ar_r, load,
):
    fetch = pltpu.make_async_copy(hblocks, blocks, load)
    fetch.start()
    r = lax.axis_index("row")
    c = lax.axis_index("col")
    core = lax.rem(r, 2)
    x = lax.rem(r // 2, 4)
    yh = r // 8
    z = c // 2
    yl = lax.rem(c, 2)
    sib_r = r + 1 - 2 * core
    yhp_r = lax.rem(r + 8, NR)
    ylp_c = c + 1 - 2 * yl
    sib = (sib_r, c)
    yhp = (yhp_r, c)
    ylp = (r, ylp_c)

    def xrow(d, h=None, k=None):
        return (yh if h is None else h) * 8 + lax.rem(x + d + 4, 4) * 2 + (core if k is None else k)

    def zcol(d, l=None):
        return lax.rem(z + d + 4, 4) * 2 + (yl if l is None else l)

    def part_of(buf, t, u, slot):
        return buf.at[t, u, :, pl.ds(pl.multiple_of(slot * LR, LR), LR)]

    upper = yh == 0
    lower = yh == 1
    yr[...] = jnp.zeros_like(yr)
    barrier = pltpu.get_barrier_semaphore()

    def greet_row(j, carry):
        pl.semaphore_signal(barrier, inc=1, device_id=(lax.rem(r + j, NR), c), device_id_type=MESH)
        return carry

    def greet_col(j, carry):
        pl.semaphore_signal(barrier, inc=1, device_id=(r, lax.rem(c + j, NC)), device_id_type=MESH)
        return carry

    lax.fori_loop(1, NR, greet_row, 0)
    lax.fori_loop(1, NC, greet_col, 0)

    cur[...] = y0[...].T
    prev[...] = jnp.zeros_like(prev)
    pl.semaphore_wait(barrier, NR - 1 + NC - 1)


    def send_block(buf, t, u, slot, dev, k):
        side = 0 if buf is vc else 1
        rcopy(
            part_of(buf, t, u, slot), part_of(buf, t, u, slot),
            ag_s.at[t, u, side], ag_r.at[t, u, k], dev,
        ).start()

    def arrived(buf, t, u, slot, k):
        rcopy(
            part_of(buf, t, u, slot), part_of(buf, t, u, slot),
            ag_s.at[t, u, 0], ag_r.at[t, u, k], sib,
        ).wait_recv()

    def blocks_of(buf, t, u, count):
        return buf.at[t, u, :, pl.ds(0, count * LR)]

    def begin(t, u, value):
        vc[t, u, :, pl.ds(pl.multiple_of(r * LR, LR), LR)] = value
        vr[t, u, :, pl.ds(pl.multiple_of(c * LR, LR), LR)] = value
        send_block(vr, t, u, c, ylp, 5)

        @pl.when(lower)
        def _():
            send_block(vc, t, u, r, yhp, 1)

        for d in (2, 1, 3):
            send_block(vc, t, u, r, (xrow(d), c), 1 + d)
            send_block(vr, t, u, c, (r, zcol(d)), 6)
        send_block(vc, t, u, r, sib, 0)

    def relay(t, u):
        arrived(vr, t, u, ylp_c, 5)
        for d in (2, 1, 3):
            send_block(vr, t, u, ylp_c, (r, zcol(d)), 6)

        @pl.when(upper)
        def _():
            arrived(vc, t, u, yhp_r, 1)
            for d in (2, 1, 3):
                send_block(vc, t, u, yhp_r, (xrow(d), c), 6 + d)
            send_block(vc, t, u, yhp_r, sib, 0)

    def pass_on(t, u):
        for d in (1, 3, 2):
            arrived(vc, t, u, xrow(-d), 1 + d)
            send_block(vc, t, u, xrow(-d), sib, 0)
        six = blocks_of(vr, t, u, 6)
        rcopy(six, six, ag_s.at[t, u, 1], ag_r.at[t, u, 6], sib).wait_recv()

    def pass_far(t, u):
        @pl.when(upper)
        def _():
            for d in (1, 3, 2):
                arrived(vc, t, u, xrow(-d, h=1 - yh), 6 + d)
                send_block(vc, t, u, xrow(-d, h=1 - yh), sib, 0)

    def wait_blocks(buf, t, u, count, side, received):
        some = blocks_of(buf, t, u, count)
        cp = rcopy(some, some, ag_s.at[t, u, side], ag_r.at[t, u, 0], sib)
        if received:
            cp.wait_recv()
        else:
            cp.wait_send()

    def gathered(t, u):
        pl.when(upper)(lambda: wait_blocks(vc, t, u, 8, 0, True))
        pl.when(lower)(lambda: wait_blocks(vc, t, u, 4, 0, True))

    def settle_gather(t, u):
        pl.when(upper)(lambda: wait_blocks(vc, t, u, 14, 0, False))
        pl.when(lower)(lambda: wait_blocks(vc, t, u, 8, 0, False))
        wait_blocks(vr, t, u, 7, 1, False)

    centre = 0.5 * (top[...] + low[...])
    halfwidth = 0.5 * (top[...] - low[...])


    def to_sib(t, u, e, d):
        return rcopy(
            ms.at[t, u, e, d, 1 - core], sr.at[t, u, e, d],
            rs_s.at[t, u, 0], rs_r.at[t, u, e * 4 + d], sib,
        )

    def along_x(t, u, e, d):
        return rcopy(
            mx.at[t, u, e, d], xr.at[t, u, e, d - 1],
            rs_s.at[t, u, 1], rs_r.at[t, u, 8 + e], (xrow(d), c),
        )

    def along_z(t, u, e, d):
        return rcopy(
            zs.at[t, u, e, d], zr.at[t, u, e, d - 1],
            rs_s.at[t, u, 2 + 3 * e], rs_r.at[t, u, 10 + e], (r, zcol(d)),
        )

    def along_y(t, u):
        return (
            rcopy(ys.at[t, u], yr.at[t, u], rs_s.at[t, u, 3], rs_r.at[t, u, 12], yhp),
            rcopy(ls.at[t, u], lr.at[t, u], rs_s.at[t, u, 4], rs_r.at[t, u, 13], ylp),
        )

    def far_z(t, u):
        return rcopy(zs.at[t, u, 1, 2], zf.at[t, u], rs_s.at[t, u, 6], rs_r.at[t, u, 14], ylp)

    def settle_reduce(t, u):
        def settle_x(own, got):
            rcopy(own, own, rs_s.at[t, u, 0], rs_r.at[t, u, 0], sib).wait_send()
            rcopy(got, got, rs_s.at[t, u, 1], rs_r.at[t, u, 4], sib).wait_send()

        @pl.when(upper)
        def _():
            settle_x(mx.at[t, u], xr.at[t, u])
            along_y(t, u)[0].wait_send()

        @pl.when(lower)
        def _():
            settle_x(mx.at[t, u, 0], xr.at[t, u, 0])

        for e in range(2):
            sent = zr.at[t, u, e, pl.ds(0, 3 - e)]
            rcopy(sent, sent, rs_s.at[t, u, 2 + 3 * e], rs_r.at[t, u, 5], sib).wait_send()
        for cp in (along_y(t, u)[1], far_z(t, u)):
            cp.wait_send()

    def products(t, u, e):
        def mirror(d):
            at = pl.multiple_of(xrow(d, h=yh if e == 0 else 1 - yh, k=0) * LR, 2 * LR)
            both = product(vr[t, u], tile[:, pl.ds(at, 2 * LR)], 1, 0)
            ms[t, u, e, d, 0] = both[:, :LR]
            ms[t, u, e, d, 1] = both[:, LR:]
            to_sib(t, u, e, d).start()

        def mirror_on(d):
            to_sib(t, u, e, d).wait_recv()
            mx[t, u, e, d] = sr[t, u, e, d] + ms[t, u, e, d, core]
            if d:
                along_x(t, u, e, d).start()

        def direct(d):
            if e:
                at = pl.multiple_of(zcol(d, l=0) * LR, 2 * LR)
                both = product(vc[t, u], tile[pl.ds(at, 2 * LR), :], 1, 1)
                zs[t, u, yl, d] = both[:, :LR]
                zs[t, u, 1 - yl, d] = both[:, LR:]
            if d == 2 and e == 0:
                far_z(t, u).wait_recv()
                zs[t, u, 0, 2] = zs[t, u, 0, 2] + zf[t, u]
            if d == 2 and e == 1:
                far_z(t, u).start()
            elif d:
                along_z(t, u, e, d).start()

        if e:
            @pl.when(upper)
            def _():
                mirror(2)
                mirror(1)

            pass_far(t, u)

            @pl.when(upper)
            def _():
                mirror(3)
                for d in (2, 1, 3):
                    mirror_on(d)

            gathered(t, u)
            for d in (2, 1, 3):
                direct(d)

            @pl.when(upper)
            def _():
                mirror(0)
                mirror_on(0)

            direct(0)
        else:
            for d in (1, 3, 2):
                mirror(d)
            for d in (1, 3):
                direct(d)
                mirror_on(d)
            mirror_on(2)
            mirror(0)
            direct(0)
            mirror_on(0)
            direct(2)

    def summed(own, got, t, u, e):
        return (own[t, u, e, 0] + got[t, u, e, 0]) + (got[t, u, e, 1] + got[t, u, e, 2])

    def arrived_x(t, u, e):
        all_x = xr.at[t, u, e]
        rcopy(all_x, all_x, rs_s.at[t, u, 1], rs_r.at[t, u, 8 + e], sib).wait_recv()

    def arrived_z(t, u, e):
        all_z = zr.at[t, u, e, pl.ds(0, 3 - e)]
        rcopy(all_z, all_z, rs_s.at[t, u, 2], rs_r.at[t, u, 10 + e], sib).wait_recv()

    def reduce(t, u):
        @pl.when(upper)
        def _():
            arrived_x(t, u, 1)
            ys[t, u] = summed(mx, xr, t, u, 1)
            along_y(t, u)[0].start()

        arrived_z(t, u, 1)
        ls[t, u] = (zs[t, u, 1, 0] + zr[t, u, 1, 0]) + zr[t, u, 1, 2]
        along_y(t, u)[1].start()

    def update(t, u):
        span = slice(u * KH, (u + 1) * KH)
        now = cur[span, :]
        own = product(now.astype(BF16), diag[...], 1, 1)
        arrived_x(t, u, 0)
        own += summed(mx, xr, t, u, 0)
        arrived_z(t, u, 0)
        own += summed(zs, zr, t, u, 0)
        pl.when(lower)(lambda: along_y(t, u)[0].wait_recv())
        own += yr[t, u]
        along_y(t, u)[1].wait_recv()
        own += lr[t, u]
        scale = jnp.where(t == 0, 1.0, 2.0).astype(F32)
        following = scale * (own - centre * now) / halfwidth - prev[span, :]
        prev[span, :] = now
        cur[span, :] = following
        begin(t + 1, u, following.astype(BF16))

    for u in range(HALF):
        begin(0, u, cur[u * KH : (u + 1) * KH, :].astype(BF16))

    @pl.when(lower)
    def _():
        vc[:, :, :, : NC * LR] = jnp.zeros((DEG + 1, HALF, KH, NC * LR), BF16)

    build_diag(onsite, diag)
    fetch.wait()
    spread, first, none = build(blocks, cols, live, pick, tile)
    column[...] = spread

    def one(i, carry):
        build_row(i, blocks, column, pick, first, none, tile)
        return carry

    early = hblocks.shape[0] // 2
    lax.fori_loop(0, early, one, 0)

    def degree(t, carry):
        for u in range(HALF):
            relay(t, u)

        @pl.when(t == 0)
        def _():
            lax.fori_loop(early, hblocks.shape[0], one, 0)

        @pl.when(t > 0)
        def _():
            for u in range(HALF):
                settle_gather(t - 1, u)
                settle_reduce(t - 1, u)

        for u in range(HALF):
            pass_on(t, u)
        for e in (1, 0):
            for u in range(HALF):
                products(t, u, e)
        for u in range(HALF):
            reduce(t, u)
        for u in range(HALF):
            update(t, u)
        return carry

    lax.fori_loop(0, DEG, degree, 0)

    mine = pl.multiple_of(r * SLAB, SLAB)

    def to_row(k):
        def step(j, carry):
            slab = pl.multiple_of(lax.rem(r + j, NR) * SLAB, SLAB)
            rcopy(
                part.at[k, pl.ds(slab, SLAB)], a1.at[k, j - 1], ar_s.at[k, 0], ar_r.at[k, 0],
                (lax.rem(r + j, NR), c),
            ).start()
            return carry

        lax.fori_loop(1, NR, step, 0)

    def to_col(k):
        rcopy(a1.at[k], a1.at[k], ar_s.at[k, 0], ar_r.at[k, 0], sib).wait_recv()
        slab = part[k, pl.ds(mine, SLAB), :]
        for j in range(NR - 1):
            slab = slab + a1[k, j]
        a2[k, c] = slab
        s2[k] = slab

        def step(j, carry):
            rcopy(
                s2.at[k], a2.at[k, c], ar_s.at[k, 1], ar_r.at[k, 1], (r, lax.rem(c + j, NC))
            ).start()
            return carry

        lax.fori_loop(1, NC, step, 0)

    def spread_out(k):
        seven = a2.at[k, pl.ds(0, NC - 1)]
        rcopy(seven, seven, ar_s.at[k, 1], ar_r.at[k, 1], sib).wait_recv()
        slab = a2[k, 0]
        for j in range(1, NC):
            slab = slab + a2[k, j]
        total[k, pl.ds(mine, SLAB), :] = slab

        def step(j, carry):
            here = total.at[k, pl.ds(mine, SLAB)]
            rcopy(here, here, ar_s.at[k, 2], ar_r.at[k, 2], (lax.rem(r + j, NR), c)).start()
            return carry

        lax.fori_loop(1, NR, step, 0)

    def others(k):
        return total.at[k, pl.ds(0, K - SLAB)]

    def collect(k):
        rcopy(others(k), others(k), ar_s.at[k, 2], ar_r.at[k, 2], sib).wait_recv()

    def settle(k):
        rcopy(a1.at[k], a1.at[k], ar_s.at[k, 0], ar_r.at[k, 0], sib).wait_send()
        seven = a2.at[k, pl.ds(0, NC - 1)]
        rcopy(seven, seven, ar_s.at[k, 1], ar_r.at[k, 1], sib).wait_send()
        rcopy(others(k), others(k), ar_s.at[k, 2], ar_r.at[k, 2], sib).wait_send()

    def three(rows, image):
        high = image.astype(BF16)
        rest = image - high.astype(F32)
        mid = rest.astype(BF16)
        low_part = (rest - mid.astype(F32)).astype(BF16)
        return product(rows, high, 1, 1) + (product(rows, mid, 1, 1) + product(rows, low_part, 1, 1))

    rounded = cur[...].astype(BF16)
    part[0] = product(rounded, rounded, 1, 1)
    for u in range(HALF):
        relay(DEG, u)
    to_row(0)
    for u in range(HALF):
        pass_on(DEG, u)
        pass_far(DEG, u)
    to_col(0)
    part[1] = three(rounded, 0.5 * product(rounded, diag[...], 1, 1))
    for u in range(HALF):
        gathered(DEG, u)
    for i in range(NC // 2):
        span = slice(i * 2 * LR, (i + 1) * 2 * LR)
        every = vc[DEG].reshape(K, NR * LR)
        image = product(every, tile[span, :], 1, 1)
        part[1] += three(vr[DEG, :, :, span].reshape(K, 2 * LR), image)
    to_row(1)
    spread_out(0)
    for u in range(HALF):
        settle_gather(DEG - 1, u)
        settle_reduce(DEG - 1, u)
        settle_gather(DEG, u)
    scale = 1.0 / (NR * NC * LR)
    inverse[...] = jnp.zeros_like(inverse)
    to_col(1)
    collect(0)
    factor[...] = total[0] * scale
    eliminate(factor, inverse, 0)
    eliminate(factor, inverse, 1)
    spread_out(1)
    eliminate(factor, inverse, 2)
    eliminate(factor, inverse, 3)
    w = inverse[...]
    inv_out[...] = w
    orb_out[...] = dot_f32(cur[...], w, 0, 1)
    settle(0)
    collect(1)
    ritz_out[...] = total[1] * scale
    settle(1)


def project(made, inverse, half, orb, proj):
    w = inverse[...]
    both = half[...]
    orb[...] = made[...]
    proj[...] = dot_nt(dot_nn(w, both + both.T), w)


def local(orbitals_in, hblocks, block_cols, live_counts, onsite, cut_low, top_bound):
    vmem = pl.BlockSpec(memory_space=pltpu.VMEM)
    anywhere = pl.BlockSpec(memory_space=pl.ANY)
    block = (KH, LR)
    steps = (DEG, HALF)
    dma = pltpu.SemaphoreType.DMA
    square = jax.ShapeDtypeStruct((K, K), F32)
    rows = jax.ShapeDtypeStruct((LR, K), F32)
    orbitals, inverse, half = pl.pallas_call(
        kernel,
        out_shape=(rows, square, square),
        in_specs=[anywhere] + [vmem] * 6,
        out_specs=(vmem, vmem, vmem),
        scratch_shapes=[
            pltpu.VMEM((NC * LR, NR * LR), BF16),
            pltpu.VMEM(hblocks.shape, BF16),
            pltpu.VMEM((NR * 16, 32 * hblocks.shape[1]), F32),
            pltpu.VMEM((hblocks.shape[0], 32 * hblocks.shape[1]), F32),
            pltpu.VMEM((LR, LR), BF16),
            pltpu.VMEM((DEG + 1, HALF, KH, NR * LR), BF16),
            pltpu.VMEM((DEG + 1, HALF, KH, NC * LR), BF16),
            pltpu.VMEM(steps + (2, 4, 2) + block, F32),
            pltpu.VMEM(steps + (2, 4) + block, F32),
            pltpu.VMEM(steps + (2, 4) + block, F32),
            pltpu.VMEM(steps + (2, 3) + block, F32),
            pltpu.VMEM(steps + (2, 4) + block, F32),
            pltpu.VMEM(steps + (2, 3) + block, F32),
            pltpu.VMEM(steps + block, F32),
            pltpu.VMEM(steps + block, F32),
            pltpu.VMEM(steps + block, F32),
            pltpu.VMEM(steps + block, F32),
            pltpu.VMEM(steps + block, F32),
            pltpu.VMEM((K, LR), F32),
            pltpu.VMEM((K, LR), F32),
            pltpu.VMEM((2, K, K), F32),
            pltpu.VMEM((2, NR - 1, SLAB, K), F32),
            pltpu.VMEM((2, SLAB, K), F32),
            pltpu.VMEM((2, NC, SLAB, K), F32),
            pltpu.VMEM((2, K, K), F32),
            pltpu.VMEM((K, K), F32),
            pltpu.VMEM((K, K), F32),
            dma((DEG + 1, HALF, 2)),
            dma((DEG + 1, HALF, 10)),
            dma((DEG, HALF, 7)),
            dma((DEG, HALF, 15)),
            dma((2, 3)),
            dma((2, 3)),
            dma,
        ],
        compiler_params=pltpu.CompilerParams(
            collective_id=0, has_side_effects=True, vmem_limit_bytes=62 * 1024 * 1024
        ),
        name="filter_and_project",
    )(
        hblocks, block_cols, live_counts.reshape(1, -1), orbitals_in, onsite,
        cut_low, top_bound,
    )
    return pl.pallas_call(
        project,
        out_shape=(rows, square),
        name="project",
    )(orbitals, inverse, half)


def solution(mesh):
    placed = (
        P(("row", "col"), None),
        P("row", "col", None),
        P("row", "col"),
        P("row", "col"),
        P(("row", "col"), None),
        P(),
        P(),
    )
    return jax.shard_map(
        local, mesh=mesh, in_specs=placed, out_specs=(P(("row", "col"), None), P()), check_vma=False
    )
```
